256 devices in a mesh: row: 32 (over x, z), col: 8 (over y, core).
Axes of the slice: x: 4, y: 4, z: 8, core: 2. Of those that a mesh axis runs over, the one named last changes fastest.
Arguments:
- kernel: float32 [2048, 65536], P('row', 'col'), may hold values from -6 to 6
- basis: float32 [65536, 128], P('col', 'row'), may hold values from -0.0234375 to 0.0234375
- responses: float32 [2048, 512], P('row', 'col'), may hold values from -6 to 6
Outputs:
- scores: float32 [2048, 128], P('row')
- loadings: float32 [128, 65536], P('row', 'col')
- weights: float32 [512, 128], P('col')
- deflated: float32 [2048, 65536], P('row', 'col')
- basis_next: float32 [2048, 128], P('row')
The draws below stay inside these ranges and needn't reach their ends.
All inputs are finite; a program needn't handle non-finite values.
Results may differ from the reference program's by a relative error of at most 0.00012.
Values sent between devices are 32-bit elements; how exact they have to be, the bound alone decides.
No kernel may reach another device: no remote copies, remote signals or barrier semaphores. Data moves between devices by JAX's collectives and lax.ppermute only.
A program may use at most 64 MiB of HBM per device.

```python
import math
import jax
import jax.numpy as jnp
from jax import lax

N = 65536
COMP = 128
M = 512
ROWS = 2048


def steps_of(own_key, dims, pieces, least, high):
    gain = 1.0
    for dim, blocks in pieces:
        steps = jax.random.uniform(jax.random.fold_in(jax.random.fold_in(own_key, 6), dim), (blocks,), jnp.float32, least / len(pieces), high / len(pieces))
        gain = gain * jnp.repeat(jnp.exp(steps), dims[dim] // blocks).reshape((-1,) + (1,) * (len(dims) - 1 - dim))
    return gain


def centred(key, dims, spread, limit, split=(), held_as=jnp.bfloat16):
    loudness = steps_of(key, dims, split, -0.22, 0.18) if split else 1.0
    result = jax.random.normal(key, dims, jnp.float32) * spread * loudness
    return jnp.minimum(jnp.maximum(result, -limit), limit).astype(held_as)


def setup_inputs(seed: int = 0) -> dict:
    key_of = jax.random.split(jax.random.key(seed), 4)
    kernel = centred(key_of[0], (ROWS, N), 1.0, 6.0, ((0, 32), (1, 8)), jnp.float32)
    basis = centred(key_of[1], (N, COMP), N ** -0.5, 0.0234375, ((0, 8), (1, 32)), jnp.float32)
    responses = centred(key_of[2], (ROWS, M), 1.0, 6.0, ((0, 32), (1, 8)), jnp.float32)
    return dict(kernel=kernel, basis=basis, responses=responses)


def reference(kernel, basis, responses):
    highest = lax.Precision.HIGHEST
    root_rows = math.sqrt(ROWS)
    projected = jnp.dot(kernel, basis, precision=highest)
    gram_mat = jnp.dot(projected.T, projected, precision=highest) / ROWS
    factor = jnp.linalg.cholesky(gram_mat)
    scores = jax.scipy.linalg.solve_triangular(factor, projected.T, lower=True).T
    loadings = jnp.dot(scores.T, kernel, precision=highest) / root_rows
    deflated = kernel - jnp.dot(scores, loadings, precision=highest) / root_rows
    weights = jnp.dot(responses.T, scores, precision=highest) / root_rows
    basis_next = jnp.dot(responses, weights, precision=highest) / math.sqrt(M)
    return (scores, loadings, weights, deflated, basis_next)
```

```python
import math

import jax
import jax.numpy as jnp
from jax import lax
from jax.sharding import Mesh
from jax.sharding import PartitionSpec as P

HIGH = lax.Precision.HIGH
HIGHEST = lax.Precision.HIGHEST
XS, ZS, YS, CS = 4, 8, 4, 2
SIZES = {"x": XS, "z": ZS, "y": YS, "c": CS}


def moved(a, axis, step):
    n = SIZES[axis]
    return lax.ppermute(a, axis, [(i, (i + step) % n) for i in range(n)])


def dot(a, b, dims, precision):
    return lax.dot_general(a, b, (dims, ((), ())), precision=precision)


def exchanged(blocks):
    out = [blocks[0]] + [None] * (XS - 1)
    for d in (1, 3, 2):
        out[-d % XS] = moved(blocks[d], "x", d)
    return out


def in_order(blocks, x):
    out = []
    for want in range(XS):
        v = blocks[want]
        for at in range(1, XS):
            v = jnp.where(x == at, blocks[(want - at) % XS], v)
        out.append(v)
    return out


def ring_gather(own):
    out = [own] + [None] * (ZS - 1)
    up = down = own
    for s in range(1, ZS // 2 + 1):
        up = moved(up, "z", 1)
        out[-s % ZS] = up
        if s < ZS // 2:
            down = moved(down, "z", -1)
            out[s] = down
    return out


def ring_scatter(parts):
    half = ZS // 2
    up, down = parts[half], parts[half + 1]
    for s in range(half - 1, -1, -1):
        up = moved(up, "z", 1)
        if s:
            up = up + parts[s]
    for s in range(half - 2, -1, -1):
        down = moved(down, "z", -1)
        if s:
            down = down + parts[-s % ZS]
    return parts[0] + (up + down)


def summed_col(v):
    v = v + moved(v, "c", 1)
    one, two, three = (moved(v, "y", d) for d in (1, 2, 3))
    return (v + two) + (one + three)


def local(kernel, basis, responses):
    rows, cols = kernel.shape
    own = basis.shape[1]
    comp = own * XS * ZS
    row_count = rows * XS * ZS
    resp_count = responses.shape[1] * YS * CS
    root_rows = math.sqrt(row_count)
    wide = cols // XS
    x, z = lax.axis_index("x"), lax.axis_index("z")

    def cut(a, j):
        return lax.dynamic_slice(a, (0, ((x + j) % XS) * wide), (a.shape[0], wide))

    basis_t = basis.T
    b_blocks = exchanged([cut(basis_t, j) for j in range(XS)])
    k_blocks = exchanged([cut(kernel, j) for j in range(XS)])
    r_blocks = exchanged([responses] * XS)
    gathered = ring_gather(jnp.concatenate(in_order(b_blocks, x), 0))
    b_all = jnp.concatenate(gathered, 0)
    k_all = jnp.concatenate(k_blocks, 0)

    proj = dot(k_all, b_all, ((1,), (1,)), HIGH)
    proj = proj + moved(proj, "c", 1)

    def turned(d):
        got = moved(proj, "x", d)
        return jnp.concatenate([got[rows * d :], got[: rows * d]], 0)

    one, two, three = (turned(d) for d in (1, 2, 3))
    proj = (proj + two) + (one + three)
    one, two, three = (moved(proj, "y", d) for d in (1, 2, 3))
    proj = (proj + two) + (one + three)

    at = lax.broadcasted_iota(jnp.int32, (comp, comp), 0)
    to = lax.broadcasted_iota(jnp.int32, (comp, comp), 1)
    group = own * XS
    home = (at // own % XS * ZS + (at // group + z) % ZS) * own + at % own
    place = (home == to).astype(jnp.float32)
    proj_abs = dot(proj, place, ((1,), (0,)), HIGHEST)

    def by_x(v):
        return jnp.concatenate(in_order([v[j * rows : (j + 1) * rows] for j in range(XS)], x), 0)

    proj_x, r_all = by_x(proj), by_x(jnp.concatenate(r_blocks, 0))
    small = jnp.concatenate([by_x(proj_abs), r_all], 1)
    gram_part = dot(proj_x, small, ((0,), (0,)), HIGHEST)
    load_part = dot(proj, k_all, ((0,), (0,)), HIGH)
    pad = jnp.zeros((comp, -(comp + r_all.shape[1]) % 128), jnp.float32)
    part = jnp.concatenate([load_part, gram_part, pad], 1)
    mine = ring_scatter([part[j * group : (j + 1) * group] for j in range(ZS)])
    total = jnp.concatenate(ring_gather(mine), 0)
    raw = total[:, :wide]
    small = dot(place, total[:, wide:], ((0,), (0,)), HIGHEST)
    gram_mat = small[:, :comp] / row_count
    resp_raw = small[:, comp : comp + r_all.shape[1]]

    factor = jnp.linalg.cholesky(gram_mat)
    inv = jax.scipy.linalg.solve_triangular(factor, jnp.eye(comp, dtype=jnp.float32), lower=True)
    inv_place = dot(inv, place, ((1,), (1,)), HIGHEST)
    scores_all = dot(proj_abs, inv, ((1,), (1,)), HIGHEST)
    scores = scores_all[:rows]
    back = dot(scores_all, inv_place, ((1,), (0,)), HIGHEST) / row_count
    weights = dot(resp_raw, inv, ((0,), (1,)), HIGHEST) / root_rows
    basis_next = summed_col(dot(responses, weights, ((1,), (0,)), HIGHEST)) / math.sqrt(resp_count)

    picks = [
        lax.dynamic_slice(inv_place, ((((x + j) % XS) * ZS + z) * own, 0), (own, comp)) for j in range(XS)
    ]
    loads = dot(jnp.concatenate(picks, 0), raw, ((1,), (0,)), HIGH) / root_rows
    rest = k_all - dot(back, raw, ((1,), (0,)), HIGH)
    d_blocks = exchanged([rest[j * rows : (j + 1) * rows] for j in range(XS)])
    l_blocks = exchanged([loads[j * own : (j + 1) * own] for j in range(XS)])

    deflated = jnp.concatenate(in_order(d_blocks, x), 1)
    loadings = jnp.concatenate(in_order(l_blocks, x), 1)
    return (scores, loadings, weights, deflated, basis_next)


def solution(mesh):
    finer = Mesh(mesh.devices.reshape(XS, ZS, YS, CS), ("x", "z", "y", "c"))
    row, col = ("x", "z"), ("y", "c")
    in_specs = (P(row, col), P(col, row), P(row, col))
    out_specs = (P(row, None), P(row, col), P(col, None), P(row, col), P(row, None))
    return jax.shard_map(local, mesh=finer, in_specs=in_specs, out_specs=out_specs, check_vma=False)
```

```python
import functools
import math

import jax
import jax.numpy as jnp
from jax import lax
from jax.experimental import pallas as pl
from jax.experimental.pallas import tpu as pltpu
from jax.sharding import Mesh
from jax.sharding import PartitionSpec as P

HIGH = lax.Precision.HIGH
HIGHEST = lax.Precision.HIGHEST
XS, ZS, YS, CS = 4, 8, 4, 2
SIZES = {"x": XS, "z": ZS, "y": YS, "c": CS}
PANEL = 8
SUB = 8


def moved(a, axis, step):
    n = SIZES[axis]
    return lax.ppermute(a, axis, [(i, (i + step) % n) for i in range(n)])


def dot(a, b, dims, precision=HIGHEST):
    return lax.dot_general(
        a, b, (dims, ((), ())), precision=precision, preferred_element_type=jnp.float32
    )


def halves(v):
    top = v.astype(jnp.bfloat16)
    return top, (v - top.astype(jnp.float32)).astype(jnp.bfloat16)


def exchanged(blocks):
    out = [blocks[0]] + [None] * (XS - 1)
    for d in (1, 3, 2):
        out[-d % XS] = moved(blocks[d], "x", d)
    return out


def in_order(blocks, x):
    out = []
    for want in range(XS):
        v = blocks[want]
        for at in range(1, XS):
            v = jnp.where(x == at, blocks[(want - at) % XS], v)
        out.append(v)
    return out


def ring_gather(own):
    out = [own] + [None] * (ZS - 1)
    half = own.shape[1] // 2
    up = down = own
    for s in range(1, ZS // 2):
        up, down = lax.optimization_barrier((moved(up, "z", 1), moved(down, "z", -1)))
        out[-s % ZS], out[s] = up, down
    left, right = moved(up[:, :half], "z", 1), moved(down[:, half:], "z", -1)
    out[ZS // 2] = (left, right)
    return out


def ring_scatter(parts):
    far = ZS // 2
    half = parts[0].shape[1] // 2
    up, down = moved(parts[far][:, :half], "z", 1), moved(parts[far][:, half:], "z", -1)
    up, down = lax.optimization_barrier((up, down))
    up = jnp.concatenate([parts[far - 1][:, :half] + up, parts[far - 1][:, half:]], 1)
    down = jnp.concatenate([parts[far + 1][:, :half], parts[far + 1][:, half:] + down], 1)
    for s in range(far - 2, -1, -1):
        up, down = lax.optimization_barrier((moved(up, "z", 1), moved(down, "z", -1)))
        if s:
            up, down = up + parts[s], down + parts[-s % ZS]
    return parts[0] + (up + down)


def summed_col(v):
    v = v + moved(v, "c", 1)
    one, two, three = (moved(v, "y", d) for d in (1, 2, 3))
    return (v + two) + (one + three)


def places(comp, own, z):
    at = lax.broadcasted_iota(jnp.int32, (comp, comp), 0)
    to = lax.broadcasted_iota(jnp.int32, (comp, comp), 1)
    group = own * XS
    home = (at // own % XS * ZS + (at // group + z) % ZS) * own + at % own
    return (home == to).astype(jnp.float32)


def stacked(blocks):
    comp, wide = blocks[0].shape[0] * ZS, blocks[0].shape[1]
    flat = []
    for b in blocks:
        flat.extend(b if isinstance(b, tuple) else (b,))

    def body(*refs):
        *ins, out = refs
        ins = iter(ins)
        for j, b in enumerate(blocks):
            rows = pl.ds(j * blocks[0].shape[0], blocks[0].shape[0])
            if isinstance(b, tuple):
                out[rows, : wide // 2] = next(ins)[...]
                out[rows, wide // 2 :] = next(ins)[...]
            else:
                out[rows, :] = next(ins)[...]

    return pl.pallas_call(
        body,
        out_shape=jax.ShapeDtypeStruct((comp, wide), jnp.float32),
        in_specs=[pl.BlockSpec(memory_space=pltpu.VMEM)] * len(flat),
        out_specs=pl.BlockSpec(memory_space=pltpu.VMEM),
        compiler_params=pltpu.CompilerParams(vmem_limit_bytes=8 << 20),
        name="stacked",
    )(*flat)


def inverse_factor(w_ref, v_ref, comp):
    row = lax.broadcasted_iota(jnp.int32, (PANEL, comp), 0)
    v_ref[...] = jnp.where(
        lax.broadcasted_iota(jnp.int32, (comp, comp), 0)
        == lax.broadcasted_iota(jnp.int32, (comp, comp), 1),
        1.0,
        0.0,
    )

    def panel(p, _):
        rows = pl.ds(pl.multiple_of(p * PANEL, PANEL), PANEL)
        w, v = w_ref[rows, :], v_ref[rows, :]
        turned = pltpu.roll(w, (comp - p * PANEL) % comp, 1)
        cols = [jnp.broadcast_to(turned[:, i : i + 1], (PANEL, comp)) for i in range(PANEL)]
        for i in range(PANEL):
            pivot = jnp.broadcast_to(cols[i][i : i + 1, :], (PANEL, comp))
            scale = lax.rsqrt(pivot)
            scale = scale * (1.5 - 0.5 * pivot * scale * scale)
            times = cols[i] * scale

            def step(a):
                b = jnp.broadcast_to(a[i : i + 1, :], (PANEL, comp)) * scale
                return jnp.where(row > i, a - times * b, jnp.where(row == i, b, a))

            w, v = step(w), step(v)
            cols = [step(c) if k > i else c for k, c in enumerate(cols)]
        v_ref[rows, :] = v
        below = lax.broadcasted_iota(jnp.int32, (comp, comp), 0) >= (p + 1) * PANEL
        change = dot(w, jnp.concatenate([w, v], 1), ((0,), (0,)))
        w_ref[...] = w_ref[...] - change[:, :comp]
        v_ref[...] = v_ref[...] - jnp.where(below, change[:, comp:], 0.0)
        return 0

    lax.fori_loop(0, comp // PANEL, panel, 0)


def finish_kernel(own, row_count, where, *refs):
    k_refs, g_refs = refs[:XS], refs[XS : XS + ZS + 1]
    proj_ref, resp_ref = refs[XS + ZS + 1 : XS + ZS + 3]
    scores_ref, weights_ref, next_ref, *d_refs = refs[XS + ZS + 3 : -4]
    w_ref, v_ref, small_ref, raw_ref = refs[-4:]
    comp = proj_ref.shape[1]
    group = own * XS
    rows, wide = k_refs[0].shape
    resp = resp_ref.shape[1]
    root_rows = math.sqrt(row_count)
    x, z = where[0], where[1]
    far = ZS // 2
    half = (g_refs[far].shape[1])
    for j in range(ZS):
        at = pl.ds(j * group, group)
        if j == far:
            raw_ref[at, :half] = g_refs[far][...]
            raw_ref[at, half:] = g_refs[far + 1][:, : wide - half]
            small_ref[at, :] = g_refs[far + 1][:, wide - half :]
        else:
            ref = g_refs[j if j < far else j + 1]
            raw_ref[at, :] = ref[:, :wide]
            small_ref[at, :] = ref[:, wide:]

    place = places(comp, own, z)
    small = dot(place, small_ref[...], ((0,), (0,)))
    w_ref[...] = small[:, :comp] * (1.0 / row_count)
    inverse_factor(w_ref, v_ref, comp)
    inv = v_ref[...]
    inv_place = dot(inv, place, ((1,), (1,)))
    scores_all = dot(proj_ref[...], inv, ((1,), (1,)))
    scores_ref[...] = scores_all[:rows]
    back = dot(scores_all, inv_place, ((1,), (0,))) * (1.0 / row_count)
    weights = dot(small[:, comp : comp + resp], inv, ((0,), (1,))) * (1.0 / root_rows)
    weights_ref[...] = weights
    next_ref[...] = dot(resp_ref[...], weights, ((1,), (0,)))

    at = lax.broadcasted_iota(jnp.int32, (XS * SUB, comp), 0)
    to = lax.broadcasted_iota(jnp.int32, (XS * SUB, comp), 1)
    wanted = (((x + at // SUB) % XS) * ZS + z) * own + at % SUB
    pick = jnp.where((wanted == to) & (at % SUB < own), 1.0, 0.0)
    picks = dot(pick, inv_place, ((1,), (0,))) * (1.0 / root_rows)
    left = []
    for j in range(XS):
        left += [back[j * rows : (j + 1) * rows], picks[j * SUB : (j + 1) * SUB]]
    left = jnp.concatenate(left, 0)
    left_top, left_rest = halves(left)
    step = 512

    def tile(t, _):
        at = pl.ds(pl.multiple_of(t * step, step), step)
        top, rest = halves(raw_ref[:, at])
        dims = ((1,), (0,))
        out = dot(left_top, top, dims, None) + (
            dot(left_top, rest, dims, None) + dot(left_rest, top, dims, None)
        )
        for j in range(XS):
            base = j * (rows + SUB)
            d_refs[j][:rows, at] = k_refs[j][:, at] - out[base : base + rows]
            d_refs[j][rows:, at] = out[base + rows : base + rows + SUB]
        return 0

    lax.fori_loop(0, wide // step, tile, 0)


def finish(where, k_blocks, g_blocks, proj, responses, own, row_count):
    rows, wide = k_blocks[0].shape
    comp = proj.shape[1]
    flat = []
    for b in g_blocks:
        flat.extend(b if isinstance(b, tuple) else (b,))
    extra = g_blocks[0].shape[1] - wide
    shape = functools.partial(jax.ShapeDtypeStruct, dtype=jnp.float32)
    vmem = pl.BlockSpec(memory_space=pltpu.VMEM)
    out_shape = [shape((rows, comp)), shape((responses.shape[1], comp)), shape((rows, comp))]
    out_shape += [shape((rows + SUB, wide))] * XS
    return pl.pallas_call(
        functools.partial(finish_kernel, own, row_count),
        out_shape=out_shape,
        in_specs=[pl.BlockSpec(memory_space=pltpu.SMEM)] + [vmem] * (XS + len(flat) + 2),
        out_specs=[vmem] * len(out_shape),
        scratch_shapes=[
            pltpu.VMEM((comp, comp), jnp.float32),
            pltpu.VMEM((comp, comp), jnp.float32),
            pltpu.VMEM((comp, extra), jnp.float32),
            pltpu.VMEM((comp, wide), jnp.float32),
        ],
        compiler_params=pltpu.CompilerParams(vmem_limit_bytes=24 << 20),
        name="finish",
    )(where, *k_blocks, *flat, proj, responses)


def local(kernel, basis, responses):
    rows, cols = kernel.shape
    own = basis.shape[1]
    comp = own * XS * ZS
    row_count = rows * XS * ZS
    resp_count = responses.shape[1] * YS * CS
    wide = cols // XS
    x, z, c = lax.axis_index("x"), lax.axis_index("z"), lax.axis_index("c")

    def cut(a, j):
        return lax.dynamic_slice(a, (0, ((x + j) % XS) * wide), (a.shape[0], wide))

    basis_t = basis.T
    b_blocks = exchanged([cut(basis_t, j) for j in range(XS)])
    k_blocks = exchanged([cut(kernel, j) for j in range(XS)])
    r_blocks = exchanged([responses] * XS)
    b_all = stacked(ring_gather(jnp.concatenate(in_order(b_blocks, x), 0)))
    k_all = jnp.concatenate(k_blocks, 0)

    proj = dot(k_all, b_all, ((1,), (1,)), HIGH).reshape(XS, CS, rows // CS, comp)
    mine = lax.dynamic_slice_in_dim(proj, c, 1, 1)
    other = lax.dynamic_slice_in_dim(proj, 1 - c, 1, 1)
    proj = mine + moved(other, "c", 1)
    one, two, three = (jnp.roll(moved(proj, "x", d), -d, 0) for d in (1, 2, 3))
    proj = (proj + two) + (one + three)
    one, two, three = (moved(proj, "y", d) for d in (1, 2, 3))
    proj = (proj + two) + (one + three)
    other = moved(proj, "c", 1)
    proj = jnp.concatenate([jnp.where(c == 0, proj, other), jnp.where(c == 0, other, proj)], 1)
    proj = proj.reshape(XS * rows, comp)

    proj_abs = dot(proj, places(comp, own, z), ((1,), (0,)))

    def by_x(v):
        return jnp.concatenate(in_order([v[j * rows : (j + 1) * rows] for j in range(XS)], x), 0)

    r_all = by_x(jnp.concatenate(r_blocks, 0))
    small = jnp.concatenate([by_x(proj_abs), r_all], 1)
    gram_part = dot(by_x(proj), small, ((0,), (0,)))
    load_part = dot(proj, k_all, ((0,), (0,)), HIGH)
    pad = jnp.zeros((comp, -(comp + r_all.shape[1]) % 256), jnp.float32)
    part = jnp.concatenate([load_part, gram_part, pad], 1)
    group = own * XS
    total = ring_scatter([part[j * group : (j + 1) * group] for j in range(ZS)])
    where = jnp.stack([x, z]).astype(jnp.int32)
    scores, weights, nxt, *d_blocks = finish(
        where, k_blocks, ring_gather(total), proj_abs, responses, own, row_count
    )
    d_blocks = exchanged(d_blocks)
    basis_next = summed_col(nxt) / math.sqrt(resp_count)
    whole = jnp.concatenate(in_order(d_blocks, x), 1)
    return (scores, whole[rows : rows + own], weights, whole[:rows], basis_next)


def solution(mesh):
    finer = Mesh(mesh.devices.reshape(XS, ZS, YS, CS), ("x", "z", "y", "c"))
    row, col = ("x", "z"), ("y", "c")
    in_specs = (P(row, col), P(col, row), P(row, col))
    out_specs = (P(row, None), P(row, col), P(col, None), P(row, col), P(row, None))
    return jax.shard_map(local, mesh=finer, in_specs=in_specs, out_specs=out_specs, check_vma=False)
```

```python
import functools
import math

import jax
import jax.numpy as jnp
from jax import lax
from jax.experimental import pallas as pl
from jax.experimental.pallas import tpu as pltpu
from jax.sharding import Mesh
from jax.sharding import PartitionSpec as P

HIGH = lax.Precision.HIGH
HIGHEST = lax.Precision.HIGHEST
XS, ZS, YS, CS = 4, 8, 4, 2
SIZES = {"x": XS, "z": ZS, "y": YS, "c": CS}
PANEL = 16
SUB = 8


def moved(a, axis, step):
    n = SIZES[axis]
    return lax.ppermute(a, axis, [(i, (i + step) % n) for i in range(n)])


def dot(a, b, dims, precision=HIGHEST):
    return lax.dot_general(
        a, b, (dims, ((), ())), precision=precision, preferred_element_type=jnp.float32
    )


def halves(v):
    top = v.astype(jnp.bfloat16)
    return top, (v - top.astype(jnp.float32)).astype(jnp.bfloat16)


def exchanged(blocks):
    out = [blocks[0]] + [None] * (XS - 1)
    for d in (1, 3, 2):
        out[-d % XS] = moved(blocks[d], "x", d)
    return out


def in_order(blocks, x):
    out = []
    for want in range(XS):
        v = blocks[want]
        for at in range(1, XS):
            v = jnp.where(x == at, blocks[(want - at) % XS], v)
        out.append(v)
    return out


def call(body, out_shapes, ins, limit, spaces=None, outs=None, scratch=()):
    vmem = pltpu.VMEM
    spaces = spaces or [vmem] * len(ins)
    outs = outs or [vmem] * len(out_shapes)
    return pl.pallas_call(
        body,
        out_shape=[jax.ShapeDtypeStruct(s, jnp.float32) for s in out_shapes],
        in_specs=[pl.BlockSpec(memory_space=m) for m in spaces],
        out_specs=[pl.BlockSpec(memory_space=m) for m in outs],
        scratch_shapes=scratch,
        compiler_params=pltpu.CompilerParams(vmem_limit_bytes=limit << 20),
    )(*ins)


def ring_gather(own):
    out = [own] + [None] * (ZS - 1)
    half = own.shape[1] // 2
    up = down = own
    for s in range(1, ZS // 2):
        up = moved(up, "z", 1)
        down = moved(down, "z", -1)
        up, down = lax.optimization_barrier((up, down))
        out[-s % ZS], out[s] = up, down
    out[ZS // 2 :] = [moved(up[:, :half], "z", 1), moved(down[:, half:], "z", -1)] + out[ZS // 2 + 1 :]
    return out


def merged_kernel(up_ref, down_ref, before_ref, after_ref, up_out, down_out):
    half = up_ref.shape[1]
    up_out[:, :half] = before_ref[:, :half] + up_ref[...]
    up_out[:, half:] = before_ref[:, half:]
    down_out[:, :half] = after_ref[:, :half]
    down_out[:, half:] = after_ref[:, half:] + down_ref[...]


def ring_scatter(parts):
    far = ZS // 2
    first, second = parts[far], parts[far + 1]
    parts = parts[: far + 1] + parts[far + 2 :]
    up, down = lax.optimization_barrier((moved(first, "z", 1), moved(second, "z", -1)))
    ends = [up, down, parts[far - 1], parts[far + 1]]
    up, down = call(merged_kernel, [parts[0].shape] * 2, ends, 4)
    for s in range(far - 2, -1, -1):
        up, down = lax.optimization_barrier((moved(up, "z", 1), moved(down, "z", -1)))
        if s:
            up, down = up + parts[s], down + parts[-s % ZS]
    return parts[0] + (up + down)


def summed_col(v):
    v = v + moved(v, "c", 1)
    v = v + lax.ppermute(v, "y", [(i, i ^ 1) for i in range(YS)])
    return v + moved(v, "y", 2)


def places(comp, own, z):
    at = lax.broadcasted_iota(jnp.int32, (comp, comp), 0)
    to = lax.broadcasted_iota(jnp.int32, (comp, comp), 1)
    group = own * XS
    home = (at // own % XS * ZS + (at // group + z) % ZS) * own + at % own
    return (home == to).astype(jnp.float32)


def stacked_kernel(*refs):
    *ins, out = refs
    deep, far = ins[0].shape[0], ZS // 2
    half, wide = ins[far].shape[1], ins[0].shape[1]
    for j in range(ZS):
        rows = pl.ds(j * deep, deep)
        if j == far:
            out[rows, :half] = ins[far][...]
            out[rows, half:wide] = ins[far + 1][...]
        else:
            out[rows, :wide] = ins[j + (j > far)][...]
    out[:, wide:] = jnp.zeros((out.shape[0], out.shape[1] - wide), jnp.float32)


def cut_kernel(k_ref, r_ref, *refs):
    outs, (held, sems) = refs[:XS], refs[XS:]
    rows, lanes = outs[0].shape
    wide = k_ref.shape[1] // XS
    copies = []
    for j in reversed(range(XS)):
        at = pl.multiple_of(lax.rem(lax.axis_index("x") + j, XS) * wide, 128)
        copies.append(
            pltpu.make_async_copy(k_ref.at[:, pl.ds(at, wide)], outs[j].at[:, pl.ds(0, wide)], sems.at[j])
        )
        copies[-1].start()
    copies.append(pltpu.make_async_copy(r_ref, held, sems.at[XS]))
    copies[-1].start()
    pad = jnp.zeros((rows, lanes - wide - r_ref.shape[1]), jnp.float32)
    copies[-1].wait()
    tail = jnp.concatenate([held[...], pad], 1)
    for j in range(XS):
        outs[j][:, wide:] = tail
    for copy in copies[:-1]:
        copy.wait()


def joined_kernel(*refs):
    blocks, (d_ref, l_ref, sems) = refs[:XS], refs[XS:]
    rows, wide = d_ref.shape[0], blocks[0].shape[1]
    copies = []
    for j in range(XS):
        at = pl.multiple_of(lax.rem(lax.axis_index("x") + j, XS) * wide, 128)
        copies.append(
            pltpu.make_async_copy(blocks[j].at[pl.ds(0, rows), :], d_ref.at[:, pl.ds(at, wide)], sems.at[j])
        )
        copies[-1].start()
    for j in range(XS):
        at = pl.multiple_of(lax.rem(lax.axis_index("x") + j, XS) * wide, 128)
        l_ref[:, pl.ds(at, wide)] = blocks[j][rows : rows + l_ref.shape[0], :]
    for copy in copies:
        copy.wait()


def parts_kernel(own, proj_ref, *refs):
    k_refs, proj_out, part_refs = refs[:XS], refs[XS], refs[XS + 1 :]
    comp = proj_ref.shape[1]
    group, far = own * XS, ZS // 2
    rows, lanes = k_refs[0].shape
    wide = lanes - comp
    half = part_refs[far].shape[1]
    x, z = lax.axis_index("x"), lax.axis_index("z")

    def put(at, value):
        end = at + value.shape[1]
        for j in range(ZS):
            v = value[j * group : (j + 1) * group]
            if j != far:
                part_refs[j + (j > far)][:, at:end] = v
            else:
                if at < half:
                    part_refs[far][:, at : min(end, half)] = v[:, : min(end, half) - at]
                if end > half:
                    part_refs[far + 1][:, max(at, half) - half : end - half] = v[:, max(at, half) - at :]

    proj = proj_ref[...]
    proj_abs = dot(proj, places(comp, own, z), ((1,), (0,)))
    proj_out[...] = proj_abs

    def by_x(v):
        return jnp.concatenate(in_order(v, x), 0)

    def split(v):
        return [v[j * rows : (j + 1) * rows] for j in range(XS)]

    right = jnp.concatenate([by_x(split(proj_abs)), by_x([k[:, wide:] for k in k_refs])], 1)
    put(wide, dot(by_x(split(proj)), right, ((0,), (0,))))
    top, rest = halves(proj)
    step = 512
    for at in range(0, wide, step):
        k_top, k_rest = halves(jnp.concatenate([k[:, at : at + step] for k in k_refs], 0))
        dims = ((0,), (0,))
        put(at, dot(top, k_top, dims, None) + (dot(top, k_rest, dims, None) + dot(rest, k_top, dims, None)))


def inverse_factor(w_ref, v_ref, comp):
    row = lax.broadcasted_iota(jnp.int32, (PANEL, comp), 0)
    v_ref[...] = jnp.where(
        lax.broadcasted_iota(jnp.int32, (comp, comp), 0)
        == lax.broadcasted_iota(jnp.int32, (comp, comp), 1),
        1.0,
        0.0,
    )

    def panel(p, _):
        rows = pl.ds(pl.multiple_of(p * PANEL, PANEL), PANEL)
        w, v = w_ref[rows, :], v_ref[rows, :]
        turned = pltpu.roll(w, (comp - p * PANEL) % comp, 1)
        cols = [jnp.broadcast_to(turned[:, i : i + 1], (PANEL, comp)) for i in range(PANEL)]
        for i in range(PANEL):
            pivot = jnp.broadcast_to(cols[i][i : i + 1, :], (PANEL, comp))
            scale = lax.rsqrt(pivot)
            times = cols[i] * scale

            def step(a):
                b = jnp.broadcast_to(a[i : i + 1, :], (PANEL, comp)) * scale
                return jnp.where(row > i, a - times * b, jnp.where(row == i, b, a))

            w, v = step(w), step(v)
            cols = [step(c) if k > i else c for k, c in enumerate(cols)]
        v_ref[rows, :] = v
        below = lax.broadcasted_iota(jnp.int32, (comp, comp), 0) >= (p + 1) * PANEL
        change = dot(w, jnp.concatenate([w, v], 1), ((0,), (0,)))
        w_ref[...] = w_ref[...] - change[:, :comp]
        v_ref[...] = v_ref[...] - jnp.where(below, change[:, comp:], 0.0)
        return 0

    lax.fori_loop(0, comp // PANEL, panel, 0)


def finish_kernel(own, row_count, *refs):
    k_refs, g_refs = refs[:XS], refs[XS : XS + ZS + 1]
    proj_ref, resp_ref = refs[XS + ZS + 1 : XS + ZS + 3]
    scores_ref, weights_ref, next_ref, *d_refs = refs[XS + ZS + 3 : -4]
    w_ref, v_ref, small_ref, raw_ref = refs[-4:]
    comp = proj_ref.shape[1]
    group = own * XS
    rows = k_refs[0].shape[0]
    wide = k_refs[0].shape[1] - comp
    resp = resp_ref.shape[1]
    root_rows = math.sqrt(row_count)
    x, z = lax.axis_index("x"), lax.axis_index("z")
    far = ZS // 2
    half = (g_refs[far].shape[1])
    for j in range(ZS):
        at = pl.ds(j * group, group)
        if j == far:
            raw_ref[at, :half] = g_refs[far][...]
            raw_ref[at, half:] = g_refs[far + 1][:, : wide - half]
            small_ref[at, :] = g_refs[far + 1][:, wide - half :]
        else:
            ref = g_refs[j if j < far else j + 1]
            raw_ref[at, :] = ref[:, :wide]
            small_ref[at, :] = ref[:, wide:]

    place = places(comp, own, z)
    small = dot(place, small_ref[...], ((0,), (0,)))
    w_ref[...] = small[:, :comp] * (1.0 / row_count)
    inverse_factor(w_ref, v_ref, comp)
    inv = v_ref[...]
    inv_place = dot(inv, place, ((1,), (1,)))
    scores_all = dot(proj_ref[...], inv, ((1,), (1,)))
    scores_ref[...] = scores_all[:rows]
    back = dot(scores_all, inv_place, ((1,), (0,))) * (1.0 / row_count)
    weights = dot(small[:, comp : comp + resp], inv, ((0,), (1,))) * (1.0 / root_rows)
    weights_ref[...] = weights
    next_ref[...] = dot(resp_ref[...], weights, ((1,), (0,)))

    at = lax.broadcasted_iota(jnp.int32, (XS * SUB, comp), 0)
    to = lax.broadcasted_iota(jnp.int32, (XS * SUB, comp), 1)
    wanted = (((x + at // SUB) % XS) * ZS + z) * own + at % SUB
    pick = jnp.where((wanted == to) & (at % SUB < own), 1.0, 0.0)
    picks = dot(pick, inv_place, ((1,), (0,))) * (1.0 / root_rows)
    left = []
    for j in range(XS):
        left += [back[j * rows : (j + 1) * rows], picks[j * SUB : (j + 1) * SUB]]
    left = jnp.concatenate(left, 0)
    left_top, left_rest = halves(left)
    step = 512

    def tile(t, _):
        at = pl.ds(pl.multiple_of(t * step, step), step)
        top, rest = halves(raw_ref[:, at])
        dims = ((1,), (0,))
        out = dot(left_top, top, dims, None) + (
            dot(left_top, rest, dims, None) + dot(left_rest, top, dims, None)
        )
        for j in range(XS):
            base = j * (rows + SUB)
            d_refs[j][:rows, at] = k_refs[j][:, at] - out[base : base + rows]
            d_refs[j][rows:, at] = out[base + rows : base + rows + SUB]
        return 0

    lax.fori_loop(0, wide // step, tile, 0)


def local(kernel, basis, responses):
    rows, cols = kernel.shape
    own = basis.shape[1]
    resp = responses.shape[1]
    comp = own * XS * ZS
    row_count = rows * XS * ZS
    resp_count = resp * YS * CS
    wide = cols // XS
    x, c = lax.axis_index("x"), lax.axis_index("c")
    hbm, vmem = pl.ANY, pltpu.VMEM
    dma = [pltpu.SemaphoreType.DMA((XS,))]

    basis_t = basis.T
    b_blocks = exchanged(
        [lax.dynamic_slice(basis_t, (0, ((x + j) % XS) * wide), (own, wide)) for j in range(XS)]
    )
    lanes = wide + comp
    k_blocks = call(
        cut_kernel,
        [(rows, lanes)] * XS,
        [pltpu.with_memory_space_constraint(a, pltpu.HBM) for a in (kernel, responses)],
        8,
        [pltpu.HBM] * 2,
        None,
        [pltpu.VMEM((rows, resp), jnp.float32), pltpu.SemaphoreType.DMA((XS + 1,))],
    )
    first = jnp.concatenate(in_order(b_blocks, x), 0)
    first, *k_blocks = lax.optimization_barrier((first, *k_blocks))
    k_blocks = exchanged(k_blocks)
    b_parts = ring_gather(first)
    (b_all,) = call(stacked_kernel, [(comp, lanes)], b_parts, 8)
    k_all = jnp.concatenate(k_blocks, 0)

    proj = dot(k_all, b_all, ((1,), (1,)), HIGH).reshape(XS, CS, rows // CS, comp)
    mine = lax.dynamic_slice_in_dim(proj, c, 1, 1)
    other = lax.dynamic_slice_in_dim(proj, 1 - c, 1, 1)
    proj = mine + moved(other, "c", 1)
    one, two, three = (jnp.roll(moved(proj, "x", d), -d, 0) for d in (1, 2, 3))
    proj = (proj + two) + (one + three)
    one, two, three = (moved(proj, "y", d) for d in (1, 2, 3))
    proj = (proj + two) + (one + three)
    other = moved(proj, "c", 1)
    proj = jnp.concatenate([jnp.where(c == 0, proj, other), jnp.where(c == 0, other, proj)], 1)
    proj = proj.reshape(XS * rows, comp)

    group, full = own * XS, lanes + comp
    shapes = [(group, full)] * (ZS + 1)
    shapes[ZS // 2 : ZS // 2 + 2] = [(group, full // 2)] * 2
    proj_abs, *parts = call(
        functools.partial(parts_kernel, own), [(XS * rows, comp)] + shapes, [proj, *k_blocks], 24
    )
    total = ring_gather(ring_scatter(parts))
    scores, weights, nxt, *d_blocks = call(
        functools.partial(finish_kernel, own, row_count),
        [(rows, comp), (resp, comp), (rows, comp)] + [(rows + SUB, wide)] * XS,
        [*k_blocks, *total, proj_abs, responses],
        24,
        None,
        None,
        [pltpu.VMEM(s, jnp.float32) for s in ((comp, comp), (comp, comp), (comp, full - wide), (comp, wide))],
    )
    d_blocks = exchanged(d_blocks)
    basis_next = summed_col(nxt) / math.sqrt(resp_count)
    deflated, loadings = call(
        joined_kernel, [(rows, cols), (own, cols)], d_blocks, 8, None, [hbm, vmem], dma
    )
    return (scores, loadings, weights, deflated, basis_next)


def solution(mesh):
    finer = Mesh(mesh.devices.reshape(XS, ZS, YS, CS), ("x", "z", "y", "c"))
    row, col = ("x", "z"), ("y", "c")
    in_specs = (P(row, col), P(col, row), P(row, col))
    out_specs = (P(row, None), P(row, col), P(col, None), P(row, col), P(row, None))

    return jax.shard_map(local, mesh=finer, in_specs=in_specs, out_specs=out_specs, check_vma=False)
```

```python
import functools
import math

import jax
import jax.numpy as jnp
from jax import lax
from jax.experimental import pallas as pl
from jax.experimental.pallas import tpu as pltpu
from jax.sharding import Mesh
from jax.sharding import PartitionSpec as P

HIGH = lax.Precision.HIGH
HIGHEST = lax.Precision.HIGHEST
XS, ZS, YS, CS = 4, 8, 4, 2
SIZES = {"x": XS, "z": ZS, "y": YS, "c": CS}
PANEL = 16
SUB = 8


def moved(a, axis, step):
    n = SIZES[axis]
    return lax.ppermute(a, axis, [(i, (i + step) % n) for i in range(n)])


def dot(a, b, dims, precision=HIGHEST):
    return lax.dot_general(
        a, b, (dims, ((), ())), precision=precision, preferred_element_type=jnp.float32
    )


def halves(v):
    top = v.astype(jnp.bfloat16)
    return top, (v - top.astype(jnp.float32)).astype(jnp.bfloat16)


def exchanged(blocks):
    out = [blocks[0]] + [None] * (XS - 1)
    for d in (1, 3, 2):
        out[-d % XS] = moved(blocks[d], "x", d)
    return out


def in_order(blocks, x):
    out = []
    for want in range(XS):
        v = blocks[want]
        for at in range(1, XS):
            v = jnp.where(x == at, blocks[(want - at) % XS], v)
        out.append(v)
    return out


def call(body, out_shapes, ins, limit, spaces=None, outs=None, scratch=()):
    vmem = pltpu.VMEM
    spaces = spaces or [vmem] * len(ins)
    outs = outs or [vmem] * len(out_shapes)
    return pl.pallas_call(
        body,
        out_shape=[jax.ShapeDtypeStruct(s, jnp.float32) for s in out_shapes],
        in_specs=[pl.BlockSpec(memory_space=m) for m in spaces],
        out_specs=[pl.BlockSpec(memory_space=m) for m in outs],
        scratch_shapes=scratch,
        compiler_params=pltpu.CompilerParams(vmem_limit_bytes=limit << 20),
    )(*ins)


def ring_gather(own):
    out = [own] + [None] * (ZS - 1)
    half = own.shape[1] // 2
    up = down = own
    for s in range(1, ZS // 2):
        up = moved(up, "z", 1)
        down = moved(down, "z", -1)
        up, down = lax.optimization_barrier((up, down))
        out[-s % ZS], out[s] = up, down
    out[ZS // 2 :] = [moved(up[:, :half], "z", 1), moved(down[:, half:], "z", -1)] + out[ZS // 2 + 1 :]
    return out


def merged_kernel(up_ref, down_ref, before_ref, after_ref, up_out, down_out):
    half = up_ref.shape[1]
    up_out[:, :half] = before_ref[:, :half] + up_ref[...]
    up_out[:, half:] = before_ref[:, half:]
    down_out[:, :half] = after_ref[:, :half]
    down_out[:, half:] = after_ref[:, half:] + down_ref[...]


def ring_scatter(parts):
    far = ZS // 2
    first, second = parts[far], parts[far + 1]
    parts = parts[: far + 1] + parts[far + 2 :]
    up, down = lax.optimization_barrier((moved(first, "z", 1), moved(second, "z", -1)))
    ends = [up, down, parts[far - 1], parts[far + 1]]
    up, down = call(merged_kernel, [parts[0].shape] * 2, ends, 4)
    for s in range(far - 2, -1, -1):
        up, down = lax.optimization_barrier((moved(up, "z", 1), moved(down, "z", -1)))
        if s:
            up, down = up + parts[s], down + parts[-s % ZS]
    return parts[0] + (up + down)


def summed_col(v):
    v = v + moved(v, "c", 1)
    v = v + lax.ppermute(v, "y", [(i, i ^ 1) for i in range(YS)])
    return v + moved(v, "y", 2)


def places(comp, own, z):
    at = lax.broadcasted_iota(jnp.int32, (comp, comp), 0)
    to = lax.broadcasted_iota(jnp.int32, (comp, comp), 1)
    group = own * XS
    home = (at // own % XS * ZS + (at // group + z) % ZS) * own + at % own
    return (home == to).astype(jnp.float32)


def stacked_kernel(*refs):
    *ins, out = refs
    deep, far = ins[0].shape[0], ZS // 2
    half, wide = ins[far].shape[1], ins[0].shape[1]
    for j in range(ZS):
        rows = pl.ds(j * deep, deep)
        if j == far:
            out[rows, :half] = ins[far][...]
            out[rows, half:wide] = ins[far + 1][...]
        else:
            out[rows, :wide] = ins[j + (j > far)][...]


def pack_kernel(b_hbm, r_hbm, *refs):
    outs, (b_ref, r_ref, sems) = refs[:XS], refs[XS:]
    copies = [pltpu.make_async_copy(r_hbm, r_ref, sems.at[0]), pltpu.make_async_copy(b_hbm, b_ref, sems.at[1])]
    for copy in copies:
        copy.start()
    for copy in copies:
        copy.wait()
    wide = b_ref.shape[1] // XS
    half = wide // 2
    r = r_ref[...]
    pairs = [
        jnp.concatenate([r[16 * i : 16 * i + 8], r[16 * i + 8 : 16 * i + 16]], 1)
        for i in range(r.shape[0] // 16)
    ]
    tail = jnp.concatenate(pairs, 1)
    for j in range(XS):
        at = pl.multiple_of(lax.rem(lax.axis_index("x") + j, XS) * wide, 128)
        outs[j][: b_ref.shape[0], :half] = b_ref[:, pl.ds(at, half)]
        outs[j][b_ref.shape[0] :, :half] = b_ref[:, pl.ds(at + half, half)]
        outs[j][:, half:] = tail


def unpack_kernel(*refs):
    ins, (b_out, r_out) = refs[:XS], refs[XS:]
    x = lax.axis_index("x")
    half, own = b_out.shape[1] // 2, b_out.shape[0] // XS
    rows = r_out.shape[0] // XS
    resp = (ins[0].shape[1] - half) * 16 // (2 * rows)
    r_out[...] = jnp.zeros(r_out.shape, jnp.float32)
    for at, block in enumerate(in_order([ref[...] for ref in ins], x)):
        b_out[at * own : (at + 1) * own, :half] = block[:own, :half]
        b_out[at * own : (at + 1) * own, half:] = block[own : 2 * own, :half]
        for i in range(rows // 16):
            pair = block[:, half + 2 * resp * i : half + 2 * resp * (i + 1)]
            r_out[at * rows + 16 * i : at * rows + 16 * i + 8, :resp] = pair[:, :resp]
            r_out[at * rows + 16 * i + 8 : at * rows + 16 * i + 16, :resp] = pair[:, resp:]


def cut_kernel(k_ref, *refs):
    outs, (held, in_sems, out_sems) = refs[:XS], refs[XS:]
    wide = outs[0].shape[1]
    ins = []
    for j in range(XS):
        at = pl.multiple_of(lax.rem(lax.axis_index("x") + j, XS) * wide, 128)
        to = held.at[j - 1] if j else outs[0]
        ins.append(pltpu.make_async_copy(k_ref.at[:, pl.ds(at, wide)], to, in_sems.at[j]))
    back = [pltpu.make_async_copy(held.at[j - 1], outs[j], out_sems.at[j - 1]) for j in range(1, XS)]
    for j in (1, 2, 3, 0):
        ins[j].start()
    for j in (1, 2, 3):
        ins[j].wait()
        back[j - 1].start()
    ins[0].wait()
    for copy in back:
        copy.wait()


def joined_kernel(*refs):
    blocks, (d_ref, l_ref, sems) = refs[:XS], refs[XS:]
    own, wide = l_ref.shape[0], d_ref.shape[1] // XS
    copies = []
    for j in range(XS):
        at = pl.multiple_of(lax.rem(lax.axis_index("x") + j, XS) * wide, 128)
        copies.append(
            pltpu.make_async_copy(blocks[j].at[:, pl.ds(0, wide)], d_ref.at[:, pl.ds(at, wide)], sems.at[j])
        )
        copies[-1].start()
    for j in range(XS):
        at = pl.multiple_of(lax.rem(lax.axis_index("x") + j, XS) * wide, 128)
        for u in range(wide // 256):
            low = blocks[j][SUB * u : SUB * u + own, wide:]
            high = blocks[j][SUB * u + own : SUB * (u + 1), wide:]
            l_ref[:, pl.ds(at + 128 * u, 128)] = low
            l_ref[:, pl.ds(at + wide // 2 + 128 * u, 128)] = high
    for copy in copies:
        copy.wait()


def parts_kernel(own, proj_ref, r_ref, *refs):
    k_refs, proj_out, part_refs = refs[:XS], refs[XS], refs[XS + 1 :]
    comp = proj_ref.shape[1]
    group, far = own * XS, ZS // 2
    rows, wide = k_refs[0].shape
    half = part_refs[far].shape[1]
    x, z = lax.axis_index("x"), lax.axis_index("z")

    def put(at, value):
        end = at + value.shape[1]
        for j in range(ZS):
            v = value[j * group : (j + 1) * group]
            if j != far:
                part_refs[j + (j > far)][:, at:end] = v
            else:
                if at < half:
                    part_refs[far][:, at : min(end, half)] = v[:, : min(end, half) - at]
                if end > half:
                    part_refs[far + 1][:, max(at, half) - half : end - half] = v[:, max(at, half) - at :]

    proj = proj_ref[...]
    proj_abs = dot(proj, places(comp, own, z), ((1,), (0,)))
    proj_out[...] = proj_abs

    def by_x(v):
        return jnp.concatenate(in_order(v, x), 0)

    def split(v):
        return [v[j * rows : (j + 1) * rows] for j in range(XS)]

    right = jnp.concatenate([by_x(split(proj_abs)), r_ref[...]], 1)
    put(wide, dot(by_x(split(proj)), right, ((0,), (0,))))
    top, rest = halves(proj)
    step = 512
    for at in range(0, wide, step):
        k_top, k_rest = halves(jnp.concatenate([k[:, at : at + step] for k in k_refs], 0))
        dims = ((0,), (0,))
        put(at, dot(top, k_top, dims, None) + (dot(top, k_rest, dims, None) + dot(rest, k_top, dims, None)))


def inverse_factor(w_ref, v_ref, comp):
    row = lax.broadcasted_iota(jnp.int32, (PANEL, comp), 0)
    whole = lax.broadcasted_iota(jnp.int32, (comp, comp), 0)
    v_ref[...] = jnp.where(whole == lax.broadcasted_iota(jnp.int32, (comp, comp), 1), 1.0, 0.0)

    def panel(p, last):
        last_w, last_v = last
        rows = pl.ds(pl.multiple_of(p * PANEL, PANEL), PANEL)
        shift = (comp - p * PANEL) % comp
        both = jnp.concatenate([last_w, last_v], 1)
        near = dot(pltpu.roll(last_w, shift, 1)[:, :PANEL], both, ((0,), (0,)))
        w, v = w_ref[rows, :] - near[:, :comp], v_ref[rows, :] - near[:, comp:]
        change = dot(last_w, both, ((0,), (0,)))
        w_ref[...] = w_ref[...] - change[:, :comp]
        v_ref[...] = v_ref[...] - jnp.where(whole >= (p + 1) * PANEL, change[:, comp:], 0.0)
        turned = pltpu.roll(w, shift, 1)
        cols = [jnp.broadcast_to(turned[:, i : i + 1], (PANEL, comp)) for i in range(PANEL)]
        for i in range(PANEL):
            scale = lax.rsqrt(jnp.broadcast_to(cols[i][i : i + 1, :], (PANEL, comp)))
            times = cols[i] * scale

            def step(a):
                b = jnp.broadcast_to(a[i : i + 1, :], (PANEL, comp)) * scale
                return jnp.where(row > i, a - times * b, jnp.where(row == i, b, a))

            w, v = step(w), step(v)
            cols = [step(c) if k > i else c for k, c in enumerate(cols)]
        v_ref[rows, :] = v
        return w, v

    zero = jnp.zeros((PANEL, comp), jnp.float32)
    lax.fori_loop(0, comp // PANEL, panel, (zero, zero))


def finish_kernel(own, row_count, *refs):
    k_refs, g_refs = refs[:XS], refs[XS : XS + ZS + 1]
    proj_ref, resp_ref = refs[XS + ZS + 1 : XS + ZS + 3]
    scores_ref, weights_ref, next_ref, *d_refs = refs[XS + ZS + 3 : -4]
    w_ref, v_ref, small_ref, raw_ref = refs[-4:]
    comp = proj_ref.shape[1]
    group = own * XS
    rows, wide = k_refs[0].shape
    resp = resp_ref.shape[1]
    root_rows = math.sqrt(row_count)
    x, z = lax.axis_index("x"), lax.axis_index("z")
    far = ZS // 2
    half = (g_refs[far].shape[1])
    for j in range(ZS):
        at = pl.ds(j * group, group)
        if j == far:
            raw_ref[at, :half] = g_refs[far][...]
            raw_ref[at, half:] = g_refs[far + 1][:, : wide - half]
            small_ref[at, :] = g_refs[far + 1][:, wide - half :]
        else:
            ref = g_refs[j if j < far else j + 1]
            raw_ref[at, :] = ref[:, :wide]
            small_ref[at, :] = ref[:, wide:]

    place = places(comp, own, z)
    small = dot(place, small_ref[...], ((0,), (0,)))
    w_ref[...] = small[:, :comp] * (1.0 / row_count)
    inverse_factor(w_ref, v_ref, comp)
    inv = v_ref[...]
    inv_place = dot(inv, place, ((1,), (1,)))
    scores_all = dot(proj_ref[...], inv, ((1,), (1,)))
    scores_ref[...] = scores_all[:rows]
    back = dot(scores_all, inv_place, ((1,), (0,))) * (1.0 / row_count)
    weights = dot(small[:, comp : comp + resp], inv, ((0,), (1,))) * (1.0 / root_rows)
    weights_ref[...] = weights
    next_ref[...] = dot(resp_ref[...], weights, ((1,), (0,)))

    at = lax.broadcasted_iota(jnp.int32, (XS * SUB, comp), 0)
    to = lax.broadcasted_iota(jnp.int32, (XS * SUB, comp), 1)
    wanted = (((x + at // SUB) % XS) * ZS + z) * own + at % own
    pick = jnp.where(wanted == to, 1.0, 0.0)
    picks = dot(pick, inv_place, ((1,), (0,))) * (1.0 / root_rows)
    left = []
    for j in range(XS):
        left += [back[j * rows : (j + 1) * rows], picks[j * SUB : (j + 1) * SUB]]
    left = jnp.concatenate(left, 0)
    left_top, left_rest = halves(left)
    step = 512
    upper = lax.broadcasted_iota(jnp.int32, (SUB, 128), 0) < own

    def tile(t, _):
        at = pl.ds(pl.multiple_of(t * step, step), step)
        top, rest = halves(raw_ref[:, at])
        dims = ((1,), (0,))
        out = dot(left_top, top, dims, None) + (
            dot(left_top, rest, dims, None) + dot(left_rest, top, dims, None)
        )
        for j in range(XS):
            base = j * (rows + SUB)
            d_refs[j][:rows, at] = k_refs[j][:, at] - out[base : base + rows]
            both = out[base + rows : base + rows + SUB]
            for u in range(step // 128):
                spot = pl.ds(pl.multiple_of((t % (wide // 2 // step) * (step // 128) + u) * SUB, SUB), SUB)
                kept = upper == (t < wide // 2 // step)
                d_refs[j][spot, wide:] = jnp.where(
                    kept, both[:, 128 * u : 128 * (u + 1)], d_refs[j][spot, wide:]
                )
        return 0

    lax.fori_loop(0, wide // step, tile, 0)


def local(kernel, basis, responses):
    rows, cols = kernel.shape
    own = basis.shape[1]
    resp = responses.shape[1]
    comp = own * XS * ZS
    row_count = rows * XS * ZS
    resp_count = resp * YS * CS
    wide = cols // XS
    c = lax.axis_index("c")
    hbm, vmem = pl.ANY, pltpu.VMEM
    dma = [pltpu.SemaphoreType.DMA((XS,))]

    packed = [(2 * own, wide // 2 + rows // 16 * 2 * resp)] * XS
    basis_t = basis.T
    b_blocks = exchanged(
        call(
            pack_kernel,
            packed,
            [pltpu.with_memory_space_constraint(a, pltpu.HBM) for a in (basis_t, responses)],
            4,
            [pltpu.HBM] * 2,
            None,
            [pltpu.VMEM(a.shape, jnp.float32) for a in (basis_t, responses)] + [pltpu.SemaphoreType.DMA((2,))],
        )
    )
    k_blocks = call(
        cut_kernel,
        [(rows, wide)] * XS,
        [pltpu.with_memory_space_constraint(kernel, pltpu.HBM)],
        8,
        [pltpu.HBM],
        [vmem] + [pltpu.HBM] * (XS - 1),
        [
            pltpu.VMEM((XS - 1, rows, wide), jnp.float32),
            pltpu.SemaphoreType.DMA((XS,)),
            pltpu.SemaphoreType.DMA((XS - 1,)),
        ],
    )
    group = own * XS
    first, r_all = call(unpack_kernel, [(group, wide), (XS * rows, comp)], b_blocks, 4)
    first, *k_blocks = lax.optimization_barrier((first, *k_blocks))
    k_blocks = exchanged(k_blocks)
    b_parts = ring_gather(first)
    (b_all,) = call(stacked_kernel, [(comp, wide)], b_parts, 8)
    k_all = jnp.concatenate(k_blocks, 0)

    proj = dot(k_all, b_all, ((1,), (1,)), HIGH).reshape(XS, CS, rows // CS, comp)
    mine = lax.dynamic_slice_in_dim(proj, c, 1, 1)
    other = lax.dynamic_slice_in_dim(proj, 1 - c, 1, 1)
    proj = mine + moved(other, "c", 1)
    one, two, three = (jnp.roll(moved(proj, "x", d), -d, 0) for d in (1, 2, 3))
    proj = (proj + two) + (one + three)
    one, two, three = (moved(proj, "y", d) for d in (1, 2, 3))
    proj = (proj + two) + (one + three)
    other = moved(proj, "c", 1)
    proj = jnp.concatenate([jnp.where(c == 0, proj, other), jnp.where(c == 0, other, proj)], 1)
    proj = proj.reshape(XS * rows, comp)

    full = wide + 2 * comp
    shapes = [(group, full)] * (ZS + 1)
    shapes[ZS // 2 : ZS // 2 + 2] = [(group, full // 2)] * 2
    proj_abs, *parts = call(
        functools.partial(parts_kernel, own), [(XS * rows, comp)] + shapes, [proj, r_all, *k_blocks], 24
    )
    total = ring_gather(ring_scatter(parts))
    scores, weights, nxt, *d_blocks = call(
        functools.partial(finish_kernel, own, row_count),
        [(rows, comp), (resp, comp), (rows, comp)] + [(rows, wide + comp)] * XS,
        [*k_blocks, *total, proj_abs, responses],
        24,
        None,
        None,
        [pltpu.VMEM(s, jnp.float32) for s in ((comp, comp), (comp, comp), (comp, full - wide), (comp, wide))],
    )
    d_blocks = exchanged(d_blocks)
    basis_next = summed_col(nxt) / math.sqrt(resp_count)
    deflated, loadings = call(joined_kernel, [(rows, cols), (own, cols)], d_blocks, 8, None, [hbm, vmem], dma)
    return (scores, loadings, weights, deflated, basis_next)


def solution(mesh):
    finer = Mesh(mesh.devices.reshape(XS, ZS, YS, CS), ("x", "z", "y", "c"))
    row, col = ("x", "z"), ("y", "c")
    in_specs = (P(row, col), P(col, row), P(row, col))
    out_specs = (P(row, None), P(row, col), P(col, None), P(row, col), P(row, None))

    return jax.shard_map(local, mesh=finer, in_specs=in_specs, out_specs=out_specs, check_vma=False)
```

```python
import functools
import math

import jax
import jax.numpy as jnp
from jax import lax
from jax.experimental import pallas as pl
from jax.experimental.pallas import tpu as pltpu
from jax.sharding import Mesh
from jax.sharding import PartitionSpec as P

HIGHEST = lax.Precision.HIGHEST
XS, ZS, YS, CS = 4, 8, 4, 2
SIZES = {"x": XS, "z": ZS, "y": YS, "c": CS}
PANEL = 16
SUB = 8


def moved(a, axis, step):
    n = SIZES[axis]
    return lax.ppermute(a, axis, [(i, (i + step) % n) for i in range(n)])


def dot(a, b, dims, precision=HIGHEST):
    return lax.dot_general(
        a, b, (dims, ((), ())), precision=precision, preferred_element_type=jnp.float32
    )


def halves(v):
    top = v.astype(jnp.bfloat16)
    return top, (v - top.astype(jnp.float32)).astype(jnp.bfloat16)


def exchanged(blocks):
    out = [blocks[0]] + [None] * (XS - 1)
    for d in (1, 3, 2):
        out[-d % XS] = moved(blocks[d], "x", d)
    return out


def in_order(blocks, x):
    out = []
    for want in range(XS):
        v = blocks[want]
        for at in range(1, XS):
            v = jnp.where(x == at, blocks[(want - at) % XS], v)
        out.append(v)
    return out


def call(body, out_shapes, ins, limit, spaces=None, outs=None, scratch=()):
    vmem = pltpu.VMEM
    spaces = spaces or [vmem] * len(ins)
    outs = outs or [vmem] * len(out_shapes)
    return pl.pallas_call(
        body,
        out_shape=[jax.ShapeDtypeStruct(s, jnp.float32) for s in out_shapes],
        in_specs=[pl.BlockSpec(memory_space=m) for m in spaces],
        out_specs=[pl.BlockSpec(memory_space=m) for m in outs],
        scratch_shapes=scratch,
        compiler_params=pltpu.CompilerParams(vmem_limit_bytes=limit << 20),
    )(*ins)


def ring_gather(own):
    out = [own] + [None] * (ZS - 1)
    up = down = own
    for s in range(1, ZS // 2):
        up = moved(up, "z", 1)
        down = moved(down, "z", -1)
        up, down = lax.optimization_barrier((up, down))
        out[-s % ZS], out[s] = up, down
    out[ZS // 2] = moved(up, "z", 1)
    return out


def merged_kernel(up_ref, down_ref, before_ref, after_ref, up_out, down_out):
    half = up_ref.shape[1]
    up_out[:, :half] = before_ref[:, :half] + up_ref[...]
    up_out[:, half:] = before_ref[:, half:]
    down_out[:, :half] = after_ref[:, :half]
    down_out[:, half:] = after_ref[:, half:] + down_ref[...]


def paired(v, axis, bit):
    return lax.ppermute(v, axis, [(i, i ^ bit) for i in range(SIZES[axis])])


def across(v):
    return lax.ppermute(v, "z", [(i, (i - 1 if i % 2 == 0 else i + 1) % ZS) for i in range(ZS)])


def ring_scatter(parts, gram):
    far = ZS // 2
    first, second = parts[far], parts[far + 1]
    parts = parts[: far + 1] + parts[far + 2 :]
    up, down = moved(first, "z", 1), moved(second, "z", -1)
    up, down, got = lax.optimization_barrier((up, down, paired(gram, "z", 1)))
    sums = [gram + got]
    ends = [up, down, parts[far - 1], parts[far + 1]]
    up, down = call(merged_kernel, [parts[0].shape] * 2, ends, 4)
    for s in range(far - 2, -1, -1):
        got = across(sums[-1]) if len(sums) % 2 else paired(sums[-1], "z", 1)
        up, down = moved(up, "z", 1), moved(down, "z", -1)
        if s:
            up, down, got = lax.optimization_barrier((up, down, got))
            up, down = up + parts[s], down + parts[-s % ZS]
        sums.append(got)
    own, one, other, opposite = sums
    return parts[0] + (up + down), (own + opposite) + (one + other)


def summed_col(v):
    v = v + moved(v, "c", 1)
    v = v + paired(v, "y", 1)
    return v + moved(v, "y", 2)


def places(comp, own, z):
    at = lax.broadcasted_iota(jnp.int32, (comp, comp), 0)
    to = lax.broadcasted_iota(jnp.int32, (comp, comp), 1)
    group = own * XS
    home = (at // own % XS * ZS + (at // group + z) % ZS) * own + at % own
    return (home == to).astype(jnp.float32)


def projected_kernel(*refs):
    k_refs, ins, (out, b_ref) = refs[:XS], refs[XS:-2], refs[-2:]
    deep, wide = ins[0].shape
    for j in range(ZS):
        b_ref[pl.ds(j * deep, deep), :] = ins[j][...]
    out[...] = jnp.zeros(out.shape, jnp.float32)
    step = 512

    def tile(t, _):
        at = pl.ds(pl.multiple_of(t * step, step), step)
        top, rest = halves(jnp.concatenate([k[:, at] for k in k_refs], 0))
        b_top, b_rest = halves(b_ref[:, at])
        dims = ((1,), (1,))
        out[...] += dot(top, b_top, dims, None) + (dot(top, b_rest, dims, None) + dot(rest, b_top, dims, None))
        return 0

    lax.fori_loop(0, wide // step, tile, 0)


def pack_kernel(b_hbm, r_hbm, *refs):
    outs, (b_ref, r_ref, sems) = refs[:XS], refs[XS:]
    copies = [pltpu.make_async_copy(r_hbm, r_ref, sems.at[0]), pltpu.make_async_copy(b_hbm, b_ref, sems.at[1])]
    for copy in copies:
        copy.start()
    for copy in copies:
        copy.wait()
    wide = b_ref.shape[1] // XS
    half = wide // 2
    r = r_ref[...]
    pairs = [
        jnp.concatenate([r[16 * i : 16 * i + 8], r[16 * i + 8 : 16 * i + 16]], 1)
        for i in range(r.shape[0] // 16)
    ]
    tail = jnp.concatenate(pairs, 1)
    for j in range(XS):
        at = pl.multiple_of(lax.rem(lax.axis_index("x") + j, XS) * wide, 128)
        outs[j][: b_ref.shape[0], :half] = b_ref[:, pl.ds(at, half)]
        outs[j][b_ref.shape[0] :, :half] = b_ref[:, pl.ds(at + half, half)]
        outs[j][:, half:] = tail


def unpack_kernel(*refs):
    ins, (b_out, r_out) = refs[:XS], refs[XS:]
    x = lax.axis_index("x")
    half, own = b_out.shape[1] // 2, b_out.shape[0] // XS
    rows = r_out.shape[0] // XS
    resp = (ins[0].shape[1] - half) * 16 // (2 * rows)
    r_out[...] = jnp.zeros(r_out.shape, jnp.float32)
    for at, block in enumerate(in_order([ref[...] for ref in ins], x)):
        b_out[at * own : (at + 1) * own, :half] = block[:own, :half]
        b_out[at * own : (at + 1) * own, half:] = block[own : 2 * own, :half]
        for i in range(rows // 16):
            pair = block[:, half + 2 * resp * i : half + 2 * resp * (i + 1)]
            r_out[at * rows + 16 * i : at * rows + 16 * i + 8, :resp] = pair[:, :resp]
            r_out[at * rows + 16 * i + 8 : at * rows + 16 * i + 16, :resp] = pair[:, resp:]


def cut_kernel(k_ref, *refs):
    outs, (held, in_sems, out_sems) = refs[:XS], refs[XS:]
    wide = outs[0].shape[1]
    ins = []
    for j in range(XS):
        at = pl.multiple_of(lax.rem(lax.axis_index("x") + j, XS) * wide, 128)
        to = held.at[j - 1] if j else outs[0]
        ins.append(pltpu.make_async_copy(k_ref.at[:, pl.ds(at, wide)], to, in_sems.at[j]))
    back = [pltpu.make_async_copy(held.at[j - 1], outs[j], out_sems.at[j - 1]) for j in range(1, XS)]
    for j in (1, 2, 3, 0):
        ins[j].start()
    for j in (1, 2, 3):
        ins[j].wait()
        back[j - 1].start()
    ins[0].wait()
    for copy in back:
        copy.wait()


def joined_kernel(*refs):
    blocks, (d_ref, l_ref, sems) = refs[:XS], refs[XS:]
    own, wide = l_ref.shape[0], d_ref.shape[1] // XS
    copies = []
    for j in range(XS):
        at = pl.multiple_of(lax.rem(lax.axis_index("x") + j, XS) * wide, 128)
        copies.append(
            pltpu.make_async_copy(blocks[j].at[:, pl.ds(0, wide)], d_ref.at[:, pl.ds(at, wide)], sems.at[j])
        )
        copies[-1].start()
    for j in range(XS):
        at = pl.multiple_of(lax.rem(lax.axis_index("x") + j, XS) * wide, 128)
        for u in range(wide // 256):
            low = blocks[j][SUB * u : SUB * u + own, wide:]
            high = blocks[j][SUB * u + own : SUB * (u + 1), wide:]
            l_ref[:, pl.ds(at + 128 * u, 128)] = low
            l_ref[:, pl.ds(at + wide // 2 + 128 * u, 128)] = high
    for copy in copies:
        copy.wait()


def parts_kernel(own, proj_ref, r_ref, *refs):
    k_refs, (proj_out, gram_out), part_refs = refs[:XS], refs[XS : XS + 2], refs[XS + 2 :]
    comp = proj_ref.shape[1]
    group, far = own * XS, ZS // 2
    rows, wide = k_refs[0].shape
    half = part_refs[far].shape[1]
    x, z = lax.axis_index("x"), lax.axis_index("z")

    proj = proj_ref[...]
    proj_abs = dot(proj, places(comp, own, z), ((1,), (0,)))
    proj_out[...] = proj_abs

    def by_x(v):
        return jnp.concatenate(in_order(v, x), 0)

    def split(v):
        return [v[j * rows : (j + 1) * rows] for j in range(XS)]

    right = jnp.concatenate([by_x(split(proj_abs)), r_ref[...]], 1)
    sums = dot(by_x(split(proj)), right, ((0,), (0,)))
    for j in range(ZS):
        tail = sums[j * group : (j + 1) * group, comp:]
        if j == far:
            part_refs[far + 1][:, wide - half :] = tail
        else:
            part_refs[j + (j > far)][:, wide:] = tail
    gram_out[...] = dot(places(comp, own, z), sums[:, :comp], ((0,), (0,)))
    top, rest = halves(proj)
    step = 512

    def tiles(t, _):
        near = pl.ds(pl.multiple_of(t * step, step), step)
        for side in range(2):
            at = pl.ds(pl.multiple_of(side * half + t * step, step), step)
            k_top, k_rest = halves(jnp.concatenate([k[:, at] for k in k_refs], 0))
            dims = ((0,), (0,))
            value = dot(top, k_top, dims, None) + (dot(top, k_rest, dims, None) + dot(rest, k_top, dims, None))
            for j in range(ZS):
                v = value[j * group : (j + 1) * group]
                if j == far:
                    part_refs[far + side][:, near] = v
                else:
                    part_refs[j + (j > far)][:, at] = v
        return 0

    lax.fori_loop(0, half // step, tiles, 0)


def inverse_factor(w_ref, v_ref, comp, first, last):
    row = lax.broadcasted_iota(jnp.int32, (PANEL, comp), 0)

    def panel(p, _):
        rows = pl.ds(pl.multiple_of(p * PANEL, PANEL), PANEL)
        w, v = w_ref[rows, :], v_ref[rows, :]
        turned = pltpu.roll(w, (comp - p * PANEL) % comp, 1)
        cols = [jnp.broadcast_to(turned[:, i : i + 1], (PANEL, comp)) for i in range(PANEL)]
        for i in range(PANEL):
            scale = lax.rsqrt(jnp.broadcast_to(cols[i][i : i + 1, :], (PANEL, comp)))
            times = cols[i] * scale

            def step(a):
                b = jnp.broadcast_to(a[i : i + 1, :], (PANEL, comp)) * scale
                return jnp.where(row > i, a - times * b, jnp.where(row == i, b, a))

            w, v = step(w), step(v)
            cols = [step(c) if k > i else c for k, c in enumerate(cols)]
        v_ref[rows, :] = v
        below = lax.broadcasted_iota(jnp.int32, (comp, comp), 0) >= (p + 1) * PANEL
        change = dot(w, jnp.concatenate([w, v], 1), ((0,), (0,)))
        w_ref[...] = w_ref[...] - change[:, :comp]
        v_ref[...] = v_ref[...] - jnp.where(below, change[:, comp:], 0.0)
        return 0

    lax.fori_loop(first, last, panel, 0)


def upper_kernel(row_count, gram_ref, w_ref, v_ref):
    comp = gram_ref.shape[0]
    w_ref[...] = gram_ref[...] * (1.0 / row_count)
    at = [lax.broadcasted_iota(jnp.int32, (comp, comp), d) for d in (0, 1)]
    v_ref[...] = jnp.where(at[0] == at[1], 1.0, 0.0)
    inverse_factor(w_ref, v_ref, comp, 0, comp // PANEL // 2)


def lower_kernel(w_in, v_in, v_ref, w_ref):
    comp = w_in.shape[0]
    w_ref[...], v_ref[...] = w_in[...], v_in[...]
    inverse_factor(w_ref, v_ref, comp, comp // PANEL // 2, comp // PANEL)


def finish_kernel(own, row_count, *refs):
    k_refs, g_refs = refs[:XS], refs[XS : XS + ZS]
    proj_ref, resp_ref, inv_ref = refs[XS + ZS : XS + ZS + 3]
    scores_ref, weights_ref, next_ref, *d_refs = refs[XS + ZS + 3 : -2]
    small_ref, raw_ref = refs[-2:]
    comp = proj_ref.shape[1]
    group = own * XS
    rows, wide = k_refs[0].shape
    resp = resp_ref.shape[1]
    root_rows = math.sqrt(row_count)
    x, z = lax.axis_index("x"), lax.axis_index("z")
    for j in range(ZS):
        at = pl.ds(j * group, group)
        raw_ref[at, :] = g_refs[j][:, :wide]
        small_ref[at, :] = g_refs[j][:, wide:]

    place = places(comp, own, z)
    small = dot(place, small_ref[...], ((0,), (0,)))
    inv = inv_ref[...]
    inv_place = dot(inv, place, ((1,), (1,)))
    scores_all = dot(proj_ref[...], inv, ((1,), (1,)))
    scores_ref[...] = scores_all[:rows]
    back = dot(scores_all, inv_place, ((1,), (0,))) * (1.0 / row_count)
    weights = dot(small[:, :resp], inv, ((0,), (1,))) * (1.0 / root_rows)
    weights_ref[...] = weights
    next_ref[...] = dot(resp_ref[...], weights, ((1,), (0,)))

    at = lax.broadcasted_iota(jnp.int32, (XS * SUB, comp), 0)
    to = lax.broadcasted_iota(jnp.int32, (XS * SUB, comp), 1)
    wanted = (((x + at // SUB) % XS) * ZS + z) * own + at % own
    pick = jnp.where(wanted == to, 1.0, 0.0)
    picks = dot(pick, inv_place, ((1,), (0,))) * (1.0 / root_rows)
    left = []
    for j in range(XS):
        left += [back[j * rows : (j + 1) * rows], picks[j * SUB : (j + 1) * SUB]]
    left = jnp.concatenate(left, 0)
    left_top, left_rest = halves(left)
    step = 512
    upper = lax.broadcasted_iota(jnp.int32, (SUB, 128), 0) < own

    def tile(t, _):
        at = pl.ds(pl.multiple_of(t * step, step), step)
        top, rest = halves(raw_ref[:, at])
        dims = ((1,), (0,))
        out = dot(left_top, top, dims, None) + (
            dot(left_top, rest, dims, None) + dot(left_rest, top, dims, None)
        )
        for j in range(XS):
            base = j * (rows + SUB)
            d_refs[j][:rows, at] = k_refs[j][:, at] - out[base : base + rows]
            both = out[base + rows : base + rows + SUB]
            for u in range(step // 128):
                spot = pl.ds(pl.multiple_of((t % (wide // 2 // step) * (step // 128) + u) * SUB, SUB), SUB)
                kept = upper == (t < wide // 2 // step)
                d_refs[j][spot, wide:] = jnp.where(
                    kept, both[:, 128 * u : 128 * (u + 1)], d_refs[j][spot, wide:]
                )
        return 0

    lax.fori_loop(0, wide // step, tile, 0)


def local(kernel, basis, responses):
    rows, cols = kernel.shape
    own = basis.shape[1]
    resp = responses.shape[1]
    comp = own * XS * ZS
    row_count = rows * XS * ZS
    resp_count = resp * YS * CS
    wide = cols // XS
    c = lax.axis_index("c")
    hbm, vmem = pl.ANY, pltpu.VMEM
    dma = [pltpu.SemaphoreType.DMA((XS,))]

    packed = [(2 * own, wide // 2 + rows // 16 * 2 * resp)] * XS
    basis_t = basis.T
    b_blocks = exchanged(
        call(
            pack_kernel,
            packed,
            [pltpu.with_memory_space_constraint(a, pltpu.HBM) for a in (basis_t, responses)],
            4,
            [pltpu.HBM] * 2,
            None,
            [pltpu.VMEM(a.shape, jnp.float32) for a in (basis_t, responses)] + [pltpu.SemaphoreType.DMA((2,))],
        )
    )
    k_blocks = call(
        cut_kernel,
        [(rows, wide)] * XS,
        [pltpu.with_memory_space_constraint(kernel, pltpu.HBM)],
        8,
        [pltpu.HBM],
        [vmem] + [pltpu.HBM] * (XS - 1),
        [
            pltpu.VMEM((XS - 1, rows, wide), jnp.float32),
            pltpu.SemaphoreType.DMA((XS,)),
            pltpu.SemaphoreType.DMA((XS - 1,)),
        ],
    )
    group = own * XS
    first, r_all = call(unpack_kernel, [(group, wide), (XS * rows, comp)], b_blocks, 4)
    first, *k_blocks = lax.optimization_barrier((first, *k_blocks))
    k_blocks = exchanged(k_blocks)
    b_parts = ring_gather(first)
    (proj,) = call(
        projected_kernel,
        [(XS * rows, comp)],
        [*k_blocks, *b_parts],
        16,
        scratch=[pltpu.VMEM((comp, wide), jnp.float32)],
    )

    proj = proj.reshape(XS, CS, rows // CS, comp)
    mine = lax.dynamic_slice_in_dim(proj, c, 1, 1)
    other = lax.dynamic_slice_in_dim(proj, 1 - c, 1, 1)
    proj = mine + moved(other, "c", 1)
    one, two, three = (jnp.roll(moved(proj, "x", d), -d, 0) for d in (1, 2, 3))
    proj = (proj + two) + (one + three)
    one, two, three = (moved(proj, "y", d) for d in (1, 2, 3))
    proj = (proj + two) + (one + three)
    other = moved(proj, "c", 1)
    proj = jnp.concatenate([jnp.where(c == 0, proj, other), jnp.where(c == 0, other, proj)], 1)
    proj = proj.reshape(XS * rows, comp)

    full = wide + comp
    half = full // 256 * 128
    shapes = [(group, full)] * (ZS + 1)
    shapes[ZS // 2 : ZS // 2 + 2] = [(group, half), (group, full - half)]
    proj_abs, gram, *parts = call(
        functools.partial(parts_kernel, own), [(XS * rows, comp), (comp, comp)] + shapes, [proj, r_all, *k_blocks], 24
    )
    mine, gram = ring_scatter(parts, gram)
    square = (comp, comp)
    state = call(functools.partial(upper_kernel, row_count), [square] * 2, [gram], 4)
    (inv,) = call(lower_kernel, [square], state, 4, scratch=[pltpu.VMEM(square, jnp.float32)])
    total = ring_gather(mine)
    scores, weights, nxt, *d_blocks = call(
        functools.partial(finish_kernel, own, row_count),
        [(rows, comp), (resp, comp), (rows, comp)] + [(rows, wide + comp)] * XS,
        [*k_blocks, *total, proj_abs, responses, inv],
        24,
        None,
        None,
        [pltpu.VMEM((comp, full - wide), jnp.float32), pltpu.VMEM((comp, wide), jnp.float32)],
    )
    d_blocks = exchanged(d_blocks)
    basis_next = summed_col(nxt) / math.sqrt(resp_count)
    deflated, loadings = call(joined_kernel, [(rows, cols), (own, cols)], d_blocks, 8, None, [hbm, vmem], dma)
    return (scores, loadings, weights, deflated, basis_next)


def solution(mesh):
    finer = Mesh(mesh.devices.reshape(XS, ZS, YS, CS), ("x", "z", "y", "c"))
    row, col = ("x", "z"), ("y", "c")
    in_specs = (P(row, col), P(col, row), P(row, col))
    out_specs = (P(row, None), P(row, col), P(col, None), P(row, col), P(row, None))

    return jax.shard_map(local, mesh=finer, in_specs=in_specs, out_specs=out_specs, check_vma=False)
```

```python
import functools
import math

import jax
import jax.numpy as jnp
from jax import lax
from jax.experimental import pallas as pl
from jax.experimental.pallas import tpu as pltpu
from jax.sharding import Mesh
from jax.sharding import PartitionSpec as P

HIGHEST = lax.Precision.HIGHEST
XS, ZS, YS, CS = 4, 8, 4, 2
SIZES = {"x": XS, "z": ZS, "y": YS, "c": CS}
PANEL = 16
SUB = 8


def moved(a, axis, step):
    n = SIZES[axis]
    return lax.ppermute(a, axis, [(i, (i + step) % n) for i in range(n)])


def dot(a, b, dims, precision=HIGHEST):
    return lax.dot_general(
        a, b, (dims, ((), ())), precision=precision, preferred_element_type=jnp.float32
    )


def halves(v):
    top = v.astype(jnp.bfloat16)
    return top, (v - top.astype(jnp.float32)).astype(jnp.bfloat16)


def exchanged(blocks):
    out = [blocks[0]] + [None] * (XS - 1)
    for d in (1, 3, 2):
        out[-d % XS] = moved(blocks[d], "x", d)
    return out


def in_order(blocks, x):
    out = []
    for want in range(XS):
        v = blocks[want]
        for at in range(1, XS):
            v = jnp.where(x == at, blocks[(want - at) % XS], v)
        out.append(v)
    return out


def call(body, out_shapes, ins, limit, spaces=None, outs=None, scratch=()):
    vmem = pltpu.VMEM
    spaces = spaces or [vmem] * len(ins)
    outs = outs or [vmem] * len(out_shapes)
    return pl.pallas_call(
        body,
        out_shape=[jax.ShapeDtypeStruct(s, jnp.float32) for s in out_shapes],
        in_specs=[pl.BlockSpec(memory_space=m) for m in spaces],
        out_specs=[pl.BlockSpec(memory_space=m) for m in outs],
        scratch_shapes=scratch,
        compiler_params=pltpu.CompilerParams(vmem_limit_bytes=limit << 20),
    )(*ins)


def ring_gather(own):
    out = [own] + [None] * (ZS - 1)
    up = down = own
    for s in range(1, ZS // 2):
        up = moved(up, "z", 1)
        down = moved(down, "z", -1)
        up, down = lax.optimization_barrier((up, down))
        out[-s % ZS], out[s] = up, down
    out[ZS // 2] = moved(up, "z", 1)
    return out


def merged_kernel(up_ref, down_ref, before_ref, after_ref, up_out, down_out):
    half = up_ref.shape[1]
    up_out[:, :half] = before_ref[:, :half] + up_ref[...]
    up_out[:, half:] = before_ref[:, half:]
    down_out[:, :half] = after_ref[:, :half]
    down_out[:, half:] = after_ref[:, half:] + down_ref[...]


def paired(v, axis, bit):
    return lax.ppermute(v, axis, [(i, i ^ bit) for i in range(SIZES[axis])])


def across(v):
    return lax.ppermute(v, "z", [(i, (i - 1 if i % 2 == 0 else i + 1) % ZS) for i in range(ZS)])


def ring_scatter(parts, gram):
    far = ZS // 2
    first, second = parts[far], parts[far + 1]
    parts = parts[: far + 1] + parts[far + 2 :]
    up, down = moved(first, "z", 1), moved(second, "z", -1)
    up, down, got = lax.optimization_barrier((up, down, paired(gram, "z", 1)))
    sums = [gram + got]
    ends = [up, down, parts[far - 1], parts[far + 1]]
    up, down = call(merged_kernel, [parts[0].shape] * 2, ends, 4)
    for s in range(far - 2, -1, -1):
        got = across(sums[-1]) if len(sums) % 2 else paired(sums[-1], "z", 1)
        up, down = moved(up, "z", 1), moved(down, "z", -1)
        if s:
            up, down, got = lax.optimization_barrier((up, down, got))
            up, down = up + parts[s], down + parts[-s % ZS]
        sums.append(got)
    own, one, other, opposite = sums
    return parts[0] + (up + down), (own + opposite) + (one + other)


def summed_col(v):
    v = v + moved(v, "c", 1)
    v = v + paired(v, "y", 1)
    return v + moved(v, "y", 2)


def places(comp, own, z):
    at = lax.broadcasted_iota(jnp.int32, (comp, comp), 0)
    to = lax.broadcasted_iota(jnp.int32, (comp, comp), 1)
    group = own * XS
    home = (at // own % XS * ZS + (at // group + z) % ZS) * own + at % own
    return (home == to).astype(jnp.float32)


def projected_kernel(*refs):
    k_refs, ins, (out, b_ref) = refs[:XS], refs[XS:-2], refs[-2:]
    deep, wide = ins[0].shape
    for j in range(ZS):
        b_ref[pl.ds(j * deep, deep), :] = ins[j][...]
    out[...] = jnp.zeros(out.shape, jnp.float32)
    step = 512

    def tile(t, _):
        at = pl.ds(pl.multiple_of(t * step, step), step)
        top, rest = halves(jnp.concatenate([k[:, at] for k in k_refs], 0))
        b_top, b_rest = halves(b_ref[:, at])
        dims = ((1,), (1,))
        out[...] += dot(top, b_top, dims, None) + (dot(top, b_rest, dims, None) + dot(rest, b_top, dims, None))
        return 0

    lax.fori_loop(0, wide // step, tile, 0)


def pack_kernel(b_hbm, r_hbm, *refs):
    outs, (b_ref, r_ref, sems) = refs[:XS], refs[XS:]
    copies = [pltpu.make_async_copy(r_hbm, r_ref, sems.at[0]), pltpu.make_async_copy(b_hbm, b_ref, sems.at[1])]
    for copy in copies:
        copy.start()
    for copy in copies:
        copy.wait()
    wide = b_ref.shape[1] // XS
    half = wide // 2
    r = r_ref[...]
    pairs = [
        jnp.concatenate([r[16 * i : 16 * i + 8], r[16 * i + 8 : 16 * i + 16]], 1)
        for i in range(r.shape[0] // 16)
    ]
    tail = jnp.concatenate(pairs, 1)
    for j in range(XS):
        at = pl.multiple_of(lax.rem(lax.axis_index("x") + j, XS) * wide, 128)
        outs[j][: b_ref.shape[0], :half] = b_ref[:, pl.ds(at, half)]
        outs[j][b_ref.shape[0] :, :half] = b_ref[:, pl.ds(at + half, half)]
        outs[j][:, half:] = tail


def unpack_kernel(*refs):
    ins, (b_out, r_out) = refs[:XS], refs[XS:]
    x = lax.axis_index("x")
    half, own = b_out.shape[1] // 2, b_out.shape[0] // XS
    rows = r_out.shape[0] // XS
    resp = (ins[0].shape[1] - half) * 16 // (2 * rows)
    r_out[...] = jnp.zeros(r_out.shape, jnp.float32)
    for at, block in enumerate(in_order([ref[...] for ref in ins], x)):
        b_out[at * own : (at + 1) * own, :half] = block[:own, :half]
        b_out[at * own : (at + 1) * own, half:] = block[own : 2 * own, :half]
        for i in range(rows // 16):
            pair = block[:, half + 2 * resp * i : half + 2 * resp * (i + 1)]
            r_out[at * rows + 16 * i : at * rows + 16 * i + 8, :resp] = pair[:, :resp]
            r_out[at * rows + 16 * i + 8 : at * rows + 16 * i + 16, :resp] = pair[:, resp:]


def cut_kernel(k_ref, *refs):
    outs, (held, in_sems, out_sems) = refs[:XS], refs[XS:]
    wide = outs[0].shape[1]
    ins = []
    for j in range(XS):
        at = pl.multiple_of(lax.rem(lax.axis_index("x") + j, XS) * wide, 128)
        to = held.at[j - 1] if j else outs[0]
        ins.append(pltpu.make_async_copy(k_ref.at[:, pl.ds(at, wide)], to, in_sems.at[j]))
    back = [pltpu.make_async_copy(held.at[j - 1], outs[j], out_sems.at[j - 1]) for j in range(1, XS)]
    for j in (1, 2, 3, 0):
        ins[j].start()
    for j in (1, 2, 3):
        ins[j].wait()
        back[j - 1].start()
    ins[0].wait()
    for copy in back:
        copy.wait()


def joined_kernel(*refs):
    blocks, (d_ref, l_ref, sems) = refs[:XS], refs[XS:]
    own, wide = l_ref.shape[0], d_ref.shape[1] // XS
    copies = []
    for j in range(XS):
        at = pl.multiple_of(lax.rem(lax.axis_index("x") + j, XS) * wide, 128)
        copies.append(
            pltpu.make_async_copy(blocks[j].at[:, pl.ds(0, wide)], d_ref.at[:, pl.ds(at, wide)], sems.at[j])
        )
        copies[-1].start()
    for j in range(XS):
        at = pl.multiple_of(lax.rem(lax.axis_index("x") + j, XS) * wide, 128)
        for u in range(wide // 256):
            low = blocks[j][SUB * u : SUB * u + own, wide:]
            high = blocks[j][SUB * u + own : SUB * (u + 1), wide:]
            l_ref[:, pl.ds(at + 128 * u, 128)] = low
            l_ref[:, pl.ds(at + wide // 2 + 128 * u, 128)] = high
    for copy in copies:
        copy.wait()


def parts_kernel(own, proj_ref, r_ref, *refs):
    k_refs, (proj_out, gram_out), part_refs = refs[:XS], refs[XS : XS + 2], refs[XS + 2 :]
    comp = proj_ref.shape[1]
    group, far = own * XS, ZS // 2
    rows, wide = k_refs[0].shape
    half = part_refs[far].shape[1]
    x, z = lax.axis_index("x"), lax.axis_index("z")

    proj = proj_ref[...]
    proj_abs = dot(proj, places(comp, own, z), ((1,), (0,)))
    proj_out[...] = proj_abs

    def by_x(v):
        return jnp.concatenate(in_order(v, x), 0)

    def split(v):
        return [v[j * rows : (j + 1) * rows] for j in range(XS)]

    right = jnp.concatenate([by_x(split(proj_abs)), r_ref[...]], 1)
    sums = dot(by_x(split(proj)), right, ((0,), (0,)))
    for j in range(ZS):
        tail = sums[j * group : (j + 1) * group, comp:]
        if j == far:
            part_refs[far + 1][:, wide - half :] = tail
        else:
            part_refs[j + (j > far)][:, wide:] = tail
    gram_out[...] = dot(places(comp, own, z), sums[:, :comp], ((0,), (0,)))
    top, rest = halves(proj)
    step = 512

    def tiles(t, _):
        near = pl.ds(pl.multiple_of(t * step, step), step)
        for side in range(2):
            at = pl.ds(pl.multiple_of(side * half + t * step, step), step)
            k_top, k_rest = halves(jnp.concatenate([k[:, at] for k in k_refs], 0))
            dims = ((0,), (0,))
            value = dot(top, k_top, dims, None) + (dot(top, k_rest, dims, None) + dot(rest, k_top, dims, None))
            for j in range(ZS):
                v = value[j * group : (j + 1) * group]
                if j == far:
                    part_refs[far + side][:, near] = v
                else:
                    part_refs[j + (j > far)][:, at] = v
        return 0

    lax.fori_loop(0, half // step, tiles, 0)


def inverse_factor(w_ref, v_ref, comp, first, last):
    row = lax.broadcasted_iota(jnp.int32, (PANEL, comp), 0)

    def panel(p, _):
        rows = pl.ds(pl.multiple_of(p * PANEL, PANEL), PANEL)
        w, v = w_ref[rows, :], v_ref[rows, :]
        turned = pltpu.roll(w, (comp - p * PANEL) % comp, 1)
        cols = [jnp.broadcast_to(turned[:, i : i + 1], (PANEL, comp)) for i in range(PANEL)]
        for i in range(PANEL):
            scale = lax.rsqrt(jnp.broadcast_to(cols[i][i : i + 1, :], (PANEL, comp)))
            times = cols[i] * scale

            def step(a):
                b = jnp.broadcast_to(a[i : i + 1, :], (PANEL, comp)) * scale
                return jnp.where(row > i, a - times * b, jnp.where(row == i, b, a))

            w, v = step(w), step(v)
            cols = [step(c) if k > i else c for k, c in enumerate(cols)]
        v_ref[rows, :] = v
        below = lax.broadcasted_iota(jnp.int32, (comp, comp), 0) >= (p + 1) * PANEL
        change = dot(w, jnp.concatenate([w, v], 1), ((0,), (0,)))
        w_ref[...] = w_ref[...] - change[:, :comp]
        v_ref[...] = v_ref[...] - jnp.where(below, change[:, comp:], 0.0)
        return 0

    lax.fori_loop(first, last, panel, 0)


def upper_kernel(row_count, gram_ref, w_ref, v_ref):
    comp = gram_ref.shape[0]
    w_ref[...] = gram_ref[...] * (1.0 / row_count)
    at = [lax.broadcasted_iota(jnp.int32, (comp, comp), d) for d in (0, 1)]
    v_ref[...] = jnp.where(at[0] == at[1], 1.0, 0.0)
    inverse_factor(w_ref, v_ref, comp, 0, comp // PANEL // 2)


def lower_kernel(own, rows, row_count, w_in, v_in, proj_ref, v_ref, scores_ref, left_ref, w_ref):
    comp = w_in.shape[0]
    x, z = lax.axis_index("x"), lax.axis_index("z")
    w_ref[...], v_ref[...] = w_in[...], v_in[...]
    inverse_factor(w_ref, v_ref, comp, comp // PANEL // 2, comp // PANEL)
    inv = v_ref[...]
    inv_place = dot(inv, places(comp, own, z), ((1,), (1,)))
    scores_all = dot(proj_ref[...], inv, ((1,), (1,)))
    scores_ref[...] = scores_all[:rows]
    back = dot(scores_all, inv_place, ((1,), (0,))) * (1.0 / row_count)
    at = lax.broadcasted_iota(jnp.int32, (XS * SUB, comp), 0)
    to = lax.broadcasted_iota(jnp.int32, (XS * SUB, comp), 1)
    wanted = (((x + at // SUB) % XS) * ZS + z) * own + at % own
    pick = jnp.where(wanted == to, 1.0, 0.0)
    picks = dot(pick, inv_place, ((1,), (0,))) * (1.0 / math.sqrt(row_count))
    for j in range(XS):
        base = j * (rows + SUB)
        left_ref[base : base + rows, :] = back[j * rows : (j + 1) * rows]
        left_ref[base + rows : base + rows + SUB, :] = picks[j * SUB : (j + 1) * SUB]


def finish_kernel(own, row_count, *refs):
    k_refs, g_refs = refs[:XS], refs[XS : XS + ZS]
    resp_ref, inv_ref, left_ref = refs[XS + ZS : XS + ZS + 3]
    weights_ref, next_ref, *d_refs = refs[XS + ZS + 3 : -2]
    small_ref, raw_ref = refs[-2:]
    comp = inv_ref.shape[1]
    group = own * XS
    rows, wide = k_refs[0].shape
    resp = resp_ref.shape[1]
    root_rows = math.sqrt(row_count)
    z = lax.axis_index("z")
    for j in range(ZS):
        at = pl.ds(j * group, group)
        raw_ref[at, :] = g_refs[j][:, :wide]
        small_ref[at, :] = g_refs[j][:, wide:]

    place = places(comp, own, z)
    small = dot(place, small_ref[...], ((0,), (0,)))
    inv = inv_ref[...]
    weights = dot(small[:, :resp], inv, ((0,), (1,))) * (1.0 / root_rows)
    weights_ref[...] = weights
    next_ref[...] = dot(resp_ref[...], weights, ((1,), (0,)))

    left_top, left_rest = halves(left_ref[...])
    step = 512
    upper = lax.broadcasted_iota(jnp.int32, (SUB, 128), 0) < own

    def tile(t, _):
        at = pl.ds(pl.multiple_of(t * step, step), step)
        top, rest = halves(raw_ref[:, at])
        dims = ((1,), (0,))
        out = dot(left_top, top, dims, None) + (
            dot(left_top, rest, dims, None) + dot(left_rest, top, dims, None)
        )
        for j in range(XS):
            base = j * (rows + SUB)
            d_refs[j][:rows, at] = k_refs[j][:, at] - out[base : base + rows]
            both = out[base + rows : base + rows + SUB]
            for u in range(step // 128):
                spot = pl.ds(pl.multiple_of((t % (wide // 2 // step) * (step // 128) + u) * SUB, SUB), SUB)
                kept = upper == (t < wide // 2 // step)
                d_refs[j][spot, wide:] = jnp.where(
                    kept, both[:, 128 * u : 128 * (u + 1)], d_refs[j][spot, wide:]
                )
        return 0

    lax.fori_loop(0, wide // step, tile, 0)


def local(kernel, basis, responses):
    rows, cols = kernel.shape
    own = basis.shape[1]
    resp = responses.shape[1]
    comp = own * XS * ZS
    row_count = rows * XS * ZS
    resp_count = resp * YS * CS
    wide = cols // XS
    c = lax.axis_index("c")
    hbm, vmem = pl.ANY, pltpu.VMEM
    dma = [pltpu.SemaphoreType.DMA((XS,))]

    packed = [(2 * own, wide // 2 + rows // 16 * 2 * resp)] * XS
    basis_t = basis.T
    b_blocks = exchanged(
        call(
            pack_kernel,
            packed,
            [pltpu.with_memory_space_constraint(a, pltpu.HBM) for a in (basis_t, responses)],
            4,
            [pltpu.HBM] * 2,
            None,
            [pltpu.VMEM(a.shape, jnp.float32) for a in (basis_t, responses)] + [pltpu.SemaphoreType.DMA((2,))],
        )
    )
    k_blocks = call(
        cut_kernel,
        [(rows, wide)] * XS,
        [pltpu.with_memory_space_constraint(kernel, pltpu.HBM)],
        8,
        [pltpu.HBM],
        [vmem] + [pltpu.HBM] * (XS - 1),
        [
            pltpu.VMEM((XS - 1, rows, wide), jnp.float32),
            pltpu.SemaphoreType.DMA((XS,)),
            pltpu.SemaphoreType.DMA((XS - 1,)),
        ],
    )
    group = own * XS
    first, r_all = call(unpack_kernel, [(group, wide), (XS * rows, comp)], b_blocks, 4)
    first, *k_blocks = lax.optimization_barrier((first, *k_blocks))
    k_blocks = exchanged(k_blocks)
    b_parts = ring_gather(first)
    (proj,) = call(
        projected_kernel,
        [(XS * rows, comp)],
        [*k_blocks, *b_parts],
        16,
        scratch=[pltpu.VMEM((comp, wide), jnp.float32)],
    )

    proj = proj.reshape(XS, CS, rows // CS, comp)
    mine = lax.dynamic_slice_in_dim(proj, c, 1, 1)
    other = lax.dynamic_slice_in_dim(proj, 1 - c, 1, 1)
    proj = mine + moved(other, "c", 1)
    one, two, three = (jnp.roll(moved(proj, "x", d), -d, 0) for d in (1, 2, 3))
    proj = (proj + two) + (one + three)
    one, two, three = (moved(proj, "y", d) for d in (1, 2, 3))
    proj = (proj + two) + (one + three)
    other = moved(proj, "c", 1)
    proj = jnp.concatenate([jnp.where(c == 0, proj, other), jnp.where(c == 0, other, proj)], 1)
    proj = proj.reshape(XS * rows, comp)

    full = wide + comp
    half = full // 256 * 128
    shapes = [(group, full)] * (ZS + 1)
    shapes[ZS // 2 : ZS // 2 + 2] = [(group, half), (group, full - half)]
    proj_abs, gram, *parts = call(
        functools.partial(parts_kernel, own),
        [(XS * rows, comp), (comp, comp)] + shapes,
        [proj, r_all, *k_blocks],
        24,
    )
    mine, gram = ring_scatter(parts, gram)
    square = (comp, comp)
    state = call(functools.partial(upper_kernel, row_count), [square] * 2, [gram], 4)
    inv, scores, left = call(
        functools.partial(lower_kernel, own, rows, row_count),
        [square, (rows, comp), (XS * (rows + SUB), comp)],
        [*state, proj_abs],
        8,
        scratch=[pltpu.VMEM(square, jnp.float32)],
    )
    total = ring_gather(mine)
    weights, nxt, *d_blocks = call(
        functools.partial(finish_kernel, own, row_count),
        [(resp, comp), (rows, comp)] + [(rows, wide + comp)] * XS,
        [*k_blocks, *total, responses, inv, left],
        24,
        None,
        None,
        [pltpu.VMEM((comp, full - wide), jnp.float32), pltpu.VMEM((comp, wide), jnp.float32)],
    )
    d_blocks = exchanged(d_blocks)
    basis_next = summed_col(nxt) / math.sqrt(resp_count)
    deflated, loadings = call(
        joined_kernel, [(rows, cols), (own, cols)], d_blocks, 8, None, [hbm, vmem], dma
    )
    return (scores, loadings, weights, deflated, basis_next)


def solution(mesh):
    finer = Mesh(mesh.devices.reshape(XS, ZS, YS, CS), ("x", "z", "y", "c"))
    row, col = ("x", "z"), ("y", "c")
    in_specs = (P(row, col), P(col, row), P(row, col))
    out_specs = (P(row, None), P(row, col), P(col, None), P(row, col), P(row, None))

    return jax.shard_map(local, mesh=finer, in_specs=in_specs, out_specs=out_specs, check_vma=False)
```
